256 devices in a mesh: row: 32 (over y, x, core), col: 8 (over z).
Axes of the slice: x: 4, y: 4, z: 8, core: 2. Of those that a mesh axis runs over, the one named last changes fastest.
Arguments:
- relief: float32 [3, 8192, 8192], P(None, 'row', 'col'), may hold values from -8 to 8
Outputs:
- level_one: float32 [3, 4096, 4096], P(None, 'row', 'col')
- level_two: float32 [3, 2048, 2048], P(None, 'row', 'col')
- level_three: float32 [3, 1024, 1024], P(None, 'row', 'col')
- level_four: float32 [3, 512, 512], P(None, 'row', 'col')
The draws below stay inside these ranges and needn't reach their ends.
All inputs are finite; a program needn't handle non-finite values.
Results may differ from the reference program's by a relative error of at most 0.00002.
Values sent between devices are 32-bit elements; how exact they have to be, the bound alone decides.
A program may use at most 64 MiB of HBM per device.

```python
import jax
import jax.numpy as jnp
from jax import lax

BANDS = 3
ROWS = 8192
COLS = 8192


def draw_relief(key, part):
    summed = jnp.zeros((BANDS, ROWS, COLS), jnp.float32)
    for octave in range(5):
        factor = 2 ** octave
        subkey = jax.random.fold_in(key, 11 + octave)
        coarse_noise = jnp.clip(jax.random.normal(subkey, (BANDS, ROWS // factor, COLS // factor), jnp.float32), -4.0, 4.0)
        summed = summed + jnp.repeat(jnp.repeat(coarse_noise, factor, 1), factor, 2)
    return jnp.clip(summed, -8.0, 8.0)


def setup_inputs(seed: int = 0) -> dict:
    key_list = jax.random.split(jax.random.key(seed), 2)
    relief = draw_relief(jax.random.fold_in(key_list[1], 71), 0)
    return dict(relief=relief)


binomial = (0.0625, 0.25, 0.375, 0.25, 0.0625)


def decimate(padded, along, extent):
    result = binomial[0] * lax.slice_in_dim(padded, 0, extent - 1, 2, along)
    for offset in range(1, 5):
        result = result + binomial[offset] * lax.slice_in_dim(padded, offset, offset + extent - 1, 2, along)
    return result


def reduce_along(field, along):
    extent = field.shape[along]
    widths = [(0, 0), (0, 0), (0, 0)]
    widths[along] = (2, 2)
    padded = jnp.pad(field, widths, mode="reflect")
    return decimate(padded, along, extent)


def reduce_level(field):
    return reduce_along(reduce_along(field, 1), 2)


def reference(relief):
    level_one = reduce_level(relief)
    level_two = reduce_level(level_one)
    level_three = reduce_level(level_two)
    level_four = reduce_level(level_three)
    return (level_one, level_two, level_three, level_four)
```

```python
import functools

import jax
import jax.numpy as jnp
import numpy as np
from jax import lax
from jax.experimental import pallas as pl
from jax.experimental.pallas import tpu as pltpu
from jax.sharding import PartitionSpec as P

MESH = pl.DeviceIdType.MESH
BINOMIAL = np.array([1, 4, 6, 4, 1]) / 16
LEVELS = 4
PAD = 8
ROW_STRIP = 32
COL_STRIP = 128
HIGHEST = lax.Precision.HIGHEST


def reduce_matrix(n, reflect):
    d = np.zeros((n // 2, n))
    for i in range(n // 2):
        for t in range(5):
            c = 2 * i - 2 + t
            if c < 0 or c >= n:
                if not reflect:
                    continue
                c = -c if c < 0 else 2 * (n - 1) - c
            d[i, c] += BINOMIAL[t]
    return d


def chain(n, reflect):
    out, m = [], np.eye(n)
    for _ in range(LEVELS):
        m = reduce_matrix(m.shape[0], reflect) @ m
        out.append(m)
    return out


def edge_parts(n):
    whole, alone = chain(3 * n, True), chain(n, False)
    places = []
    for p in range(3):
        parts = []
        for k in range(LEVELS):
            m = n >> (k + 1)
            mine = whole[k][:, p * n : (p + 1) * n]
            own = mine[p * m : (p + 1) * m] - alone[k]
            assert not own[2:-1].any()
            up = mine[(p + 1) * m : (p + 1) * m + 2] if p < 2 else np.zeros((2, n))
            down = mine[p * m - 1 : p * m] if p > 0 else np.zeros((1, n))
            parts.append((up, down, own[:2], own[-1:]))
        places.append(parts)
    return places


def ends(rows, strip):
    return np.concatenate([rows[:, :strip], rows[:, -strip:]], 1)


def tables():
    places = edge_parts(256)
    row_table = np.zeros((3, 32, 2 * ROW_STRIP), np.float32)
    col_table = np.zeros((3, 24 * LEVELS, 2 * COL_STRIP), np.float32)
    for p, parts in enumerate(places):
        for k, (up, down, first, last) in enumerate(parts):
            row_table[p, 2 * k : 2 * k + 2] = ends(up, ROW_STRIP)
            row_table[p, 8 + k] = ends(down, ROW_STRIP)[0]
            row_table[p, 16 + 2 * k : 18 + 2 * k] = ends(first, ROW_STRIP)
            row_table[p, 24 + k] = ends(last, ROW_STRIP)[0]
            col_table[p, 24 * k : 24 * k + 2] = ends(up, COL_STRIP)
            col_table[p, 24 * k + 15] = ends(down, COL_STRIP)[0]
            col_table[p, 24 * k + 16 : 24 * k + 18] = ends(first, COL_STRIP)
            col_table[p, 24 * k + 23] = ends(last, COL_STRIP)[0]
    return row_table, col_table


def split(a):
    high = a.astype(jnp.bfloat16)
    return high, (a - high.astype(jnp.float32)).astype(jnp.bfloat16)


def dot_split(a, weights):
    high, low = split(a)
    dot = functools.partial(jnp.dot, preferred_element_type=jnp.float32)
    return dot(high, weights) + dot(low, weights)


def place(index, count):
    return jnp.where(index == 0, 0, jnp.where(index == count - 1, 2, 1))


def pyramid_kernel(
    rows_n, cols_n, x_hbm, rt_hbm, ct_hbm, c1_hbm, c12_hbm, c3_hbm, c4_hbm,
    o1, o2, o3, o4,
    x, y1, y2, y3, y4, rt, ct, c1, c12, c3, c4,
    zsend_up, zsend_down, zown, zfrom_low, zfrom_high,
    vsend_up, vsend_down, vown, vfrom_low, vfrom_high,
    x_sem, t_sem, z_sem, v_sem,
):
    bands, height, width = x_hbm.shape
    r, c = lax.axis_index("row"), lax.axis_index("col")
    has_low_row, has_high_row = r > 0, r < rows_n - 1
    has_low_col, has_high_col = c > 0, c < cols_n - 1
    ys = (y1, y2, y3, y4)
    fields = (x,) + ys

    barrier = pltpu.get_barrier_semaphore()
    for axis, has, step in (
        ("row", has_low_row, -1), ("row", has_high_row, 1), ("col", has_low_col, -1), ("col", has_high_col, 1)
    ):

        @pl.when(has)
        def _(axis=axis, step=step):
            pl.semaphore_signal(
                barrier, inc=1, device_id={axis: lax.axis_index(axis) + step}, device_id_type=MESH
            )

    def load(source, target, sem):
        copy = pltpu.make_async_copy(source, target, sem)
        copy.start()
        return copy

    row_copy = load(rt_hbm.at[place(r, rows_n)], rt, t_sem.at[0])
    tiles = width // 128

    def load_rows(b, begin, end, sem):
        return [
            load(
                x_hbm.at[b, begin:end, 128 * i : 128 * i + 128],
                x.at[b, i, PAD + begin : PAD + end],
                sem.at[i],
            )
            for i in range(tiles)
        ]

    strips = [
        load_rows(b, 0, ROW_STRIP, x_sem.at[0, b])
        + load_rows(b, height - ROW_STRIP, height, x_sem.at[1, b])
        for b in range(bands)
    ]
    middles = [load_rows(b, ROW_STRIP, height - ROW_STRIP, x_sem.at[2, b]) for b in range(bands)]
    rest = [
        load(ct_hbm.at[place(c, cols_n)], ct, t_sem.at[1]),
        load(c1_hbm, c1, t_sem.at[2]),
        load(c12_hbm, c12, t_sem.at[3]),
        load(c3_hbm, c3, t_sem.at[4]),
        load(c4_hbm, c4, t_sem.at[5]),
    ]

    for field in fields[:LEVELS]:
        size = field.shape[2] - 2 * PAD
        zeros = jnp.zeros((bands, tiles, PAD, 128), jnp.float32)
        field[:, :, 0:PAD] = zeros
        field[:, :, PAD + size :] = zeros

    def across(field, b, begin, end, lanes=range(tiles)):
        return jnp.concatenate([field[b, i, PAD + begin : PAD + end] for i in lanes], 1)

    row_copy.wait()
    for b in range(bands):
        for copy in strips[b]:
            copy.wait()
        strip = jnp.concatenate(
            [across(x, b, 0, ROW_STRIP), across(x, b, height - ROW_STRIP, height)], 0
        )
        z = jnp.dot(rt[...], strip, precision=HIGHEST, preferred_element_type=jnp.float32)
        zsend_up[b] = z[0:8]
        zsend_down[b] = z[8:16]
        zown[b] = z[16:32]

    neighbours = (
        has_low_row.astype(jnp.int32)
        + has_high_row.astype(jnp.int32)
        + has_low_col.astype(jnp.int32)
        + has_high_col.astype(jnp.int32)
    )
    pl.semaphore_wait(barrier, neighbours)

    def exchange(axis, has_low, has_high, up, down, from_low, from_high, sem):
        here = lax.axis_index(axis)
        to_high = pltpu.make_async_remote_copy(
            up, from_low, sem.at[0], sem.at[1], device_id={axis: here + 1}, device_id_type=MESH
        )
        to_low = pltpu.make_async_remote_copy(
            down, from_high, sem.at[2], sem.at[3], device_id={axis: here - 1}, device_id_type=MESH
        )
        pl.when(has_high)(to_high.start)
        pl.when(has_low)(to_low.start)

        def arrive():
            pl.when(has_low)(to_high.wait_recv)
            pl.when(has_high)(to_low.wait_recv)

        def sent():
            pl.when(has_high)(to_high.wait_send)
            pl.when(has_low)(to_low.wait_send)

        return arrive, sent

    z_arrive, z_sent = exchange(
        "row", has_low_row, has_high_row, zsend_up, zsend_down, zfrom_low, zfrom_high, z_sem
    )

    for b in range(bands):
        for copy in middles[b]:
            copy.wait()

        def reduce_tile(i, carry, b=b):
            for source, target in zip(fields[:LEVELS], ys):
                size = target.shape[2] - 2 * PAD
                tap = [source[b, i, pl.ds(PAD - 2 + t, size, stride=2)] for t in range(5)]
                target[b, i, PAD : PAD + size] = (
                    0.0625 * (tap[0] + tap[4]) + 0.25 * (tap[1] + tap[3]) + 0.375 * tap[2]
                )
            return carry

        lax.fori_loop(0, tiles, reduce_tile, 0)

    z_arrive()
    for b in range(bands):
        first = jnp.where(has_low_row, zfrom_low[b], 0.0) + zown[b, 0:8]
        last = jnp.where(has_high_row, zfrom_high[b], 0.0) + zown[b, 8:16]
        for k, y in enumerate(ys):
            size = y.shape[2] - 2 * PAD
            for i in range(tiles):
                lanes = slice(128 * i, 128 * i + 128)
                y[b, i, PAD : PAD + 2] = y[b, i, PAD : PAD + 2] + first[2 * k : 2 * k + 2, lanes]
                end = slice(PAD + size - 1, PAD + size)
                y[b, i, end] = y[b, i, end] + last[k : k + 1, lanes]

    def rows_of(b, levels, lanes=range(tiles)):
        return jnp.concatenate([across(ys[k], b, 0, height >> (k + 1), lanes) for k in levels], 0)

    for copy in rest:
        copy.wait()
    lane = lax.broadcasted_iota(jnp.int32, (24, height), 1)
    for b in range(bands):
        edge = rows_of(b, range(LEVELS), (0, tiles - 1))
        edge = jnp.concatenate([edge, jnp.zeros((height >> LEVELS, 2 * COL_STRIP), jnp.float32)], 0)
        v = lax.dot_general(
            ct[...], edge, (((1,), (1,)), ((), ())), precision=HIGHEST, preferred_element_type=jnp.float32
        )
        picked = v[72:96]
        for k in range(LEVELS - 2, -1, -1):
            picked = jnp.where(lane < height - (height >> (k + 1)), v[24 * k : 24 * k + 24], picked)
        vsend_up[b] = picked[0:8]
        vsend_down[b] = picked[8:16]
        vown[b] = picked[16:24]
    v_arrive, v_sent = exchange(
        "col", has_low_col, has_high_col, vsend_up, vsend_down, vfrom_low, vfrom_high, v_sem
    )

    half = width // 2
    for b in range(bands):
        high, low = split(rows_of(b, (0,)))
        dot = functools.partial(jnp.dot, preferred_element_type=jnp.float32)
        o1[b, :, 0 : half // 2] = dot(high[:, : half + 128], c1[0]) + dot(low[:, : half + 128], c1[0])
        o1[b, :, half // 2 :] = dot(high[:, half - 128 :], c1[1]) + dot(low[:, half - 128 :], c1[1])
        two = dot_split(rows_of(b, range(1, LEVELS)), c12[...])
        o2[b] = two[: height // 4]
        three = dot_split(two[height // 4 :], c3[...])
        o3[b] = three[: height // 8]
        o4[b] = dot_split(three[height // 8 :], c4[...])[:, : width >> 4]

    v_arrive()
    at = lax.broadcasted_iota(jnp.int32, (128, 128), 1)
    for b in range(bands):
        edge = (
            jnp.where(has_low_col, vfrom_low[b], 0.0)
            + jnp.where(has_high_col, vfrom_high[b], 0.0)
            + vown[b]
        )
        for part, levels in ((0, (0,)), (1, (1, 2, 3))):
            square = jnp.concatenate(
                [edge[:, 128 * part : 128 * part + 128], jnp.zeros((120, 128), jnp.float32)], 0
            ).T
            start = 0
            for k in levels:
                out = (o1, o2, o3, o4)[k]
                size, across = out.shape[1:]
                cells = square[start : start + size]
                start += size
                tile = min(across, 128)
                first = jnp.where(at[:size] < 2, cells, 0.0)[:, :tile]
                last = jnp.where(at[:size] == tile - 1, pltpu.roll(cells, tile - 8, 1), 0.0)[:, :tile]
                out[b, :, 0:tile] = out[b, :, 0:tile] + first
                out[b, :, across - tile :] = out[b, :, across - tile :] + last
    z_sent()
    v_sent()


def store_kernel(*refs):
    sources, targets, sem = refs[:LEVELS], refs[LEVELS : 2 * LEVELS], refs[2 * LEVELS]
    copies = [pltpu.make_async_copy(s, t, sem.at[k]) for k, (s, t) in enumerate(zip(sources, targets))]
    for copy in copies:
        copy.start()
    for copy in copies:
        copy.wait()


def solution(mesh):
    rows_n, cols_n = mesh.shape["row"], mesh.shape["col"]
    row_table, col_table = tables()

    def local(relief):
        bands, height, width = relief.shape
        f32, bf16 = jnp.float32, jnp.bfloat16
        half = width // 2
        one = reduce_matrix(width, False).T
        c1 = np.stack([one[: half + 128, : half // 2], one[half - 128 :, half // 2 :]])
        c12 = chain(width, False)[1].T
        c3 = reduce_matrix(width // 4, False).T
        c4 = np.zeros((width // 8, 128))
        c4[:, : width // 16] = reduce_matrix(width // 8, False).T
        consts = [jnp.asarray(row_table), jnp.asarray(col_table)]
        consts += [jnp.asarray(a, bf16) for a in (c1, c12, c3, c4)]
        shapes = [(bands, height >> k, width >> k) for k in range(1, LEVELS + 1)]

        vmem = lambda *shape, dtype=f32: pltpu.VMEM(shape, dtype)
        scratch = [vmem(bands, width // 128, (height >> k) + 2 * PAD, 128) for k in range(LEVELS + 1)]
        scratch += [
            vmem(*row_table.shape[1:]), vmem(*col_table.shape[1:]),
            vmem(*c1.shape, dtype=bf16), vmem(*c12.shape, dtype=bf16),
            vmem(*c3.shape, dtype=bf16), vmem(*c4.shape, dtype=bf16),
            vmem(bands, 8, width), vmem(bands, 8, width), vmem(bands, 16, width),
            vmem(bands, 8, width), vmem(bands, 8, width),
            vmem(bands, 8, height), vmem(bands, 8, height), vmem(bands, 8, height),
            vmem(bands, 8, height), vmem(bands, 8, height),
            pltpu.SemaphoreType.DMA((3, bands, width // 128)), pltpu.SemaphoreType.DMA((6,)),
            pltpu.SemaphoreType.DMA((4,)), pltpu.SemaphoreType.DMA((4,)),
        ]
        held = pl.pallas_call(
            functools.partial(pyramid_kernel, rows_n, cols_n),
            out_shape=[jax.ShapeDtypeStruct(s, f32) for s in shapes],
            in_specs=[pl.BlockSpec(memory_space=pltpu.HBM)] * 7,
            out_specs=[pl.BlockSpec(memory_space=pltpu.VMEM)] * LEVELS,
            scratch_shapes=scratch,
            compiler_params=pltpu.CompilerParams(
                collective_id=0, has_side_effects=True, vmem_limit_bytes=40 << 20
            ),
            name="pyramid",
        )(*[pltpu.with_memory_space_constraint(a, pltpu.HBM) for a in (relief, *consts)])
        return pl.pallas_call(
            store_kernel,
            out_shape=[jax.ShapeDtypeStruct(s, f32) for s in shapes],
            in_specs=[pl.BlockSpec(memory_space=pltpu.VMEM)] * LEVELS,
            out_specs=[pl.BlockSpec(memory_space=pltpu.HBM)] * LEVELS,
            scratch_shapes=[pltpu.SemaphoreType.DMA((LEVELS,))],
            compiler_params=pltpu.CompilerParams(vmem_limit_bytes=16 << 20),
            name="store",
        )(*held)

    spec = P(None, "row", "col")
    return jax.shard_map(local, mesh=mesh, in_specs=(spec,), out_specs=(spec,) * LEVELS, check_vma=False)
```

```python
import functools

import jax
import jax.numpy as jnp
import numpy as np
from jax import lax
from jax.experimental import pallas as pl
from jax.experimental.pallas import tpu as pltpu
from jax.sharding import PartitionSpec as P

MESH = pl.DeviceIdType.MESH
BINOMIAL = np.array([1, 4, 6, 4, 1]) / 16
LEVELS = 4
PAD = 8
ROW_STRIP = 32
COL_STRIP = 64
UNROLL = 4


def reduce_matrix(n, reflect):
    d = np.zeros((n // 2, n))
    for i in range(n // 2):
        for t in range(5):
            c = 2 * i - 2 + t
            if c < 0 or c >= n:
                if not reflect:
                    continue
                c = -c if c < 0 else 2 * (n - 1) - c
            d[i, c] += BINOMIAL[t]
    return d


def chain(n, reflect):
    out, m = [], np.eye(n)
    for _ in range(LEVELS):
        m = reduce_matrix(m.shape[0], reflect) @ m
        out.append(m)
    return out


def edge_parts(n):
    whole, alone = chain(3 * n, True), chain(n, False)
    places = []
    for p in range(3):
        parts = []
        for k in range(LEVELS):
            m = n >> (k + 1)
            mine = whole[k][:, p * n : (p + 1) * n]
            own = mine[p * m : (p + 1) * m] - alone[k]
            assert not own[2:-1].any()
            up = mine[(p + 1) * m : (p + 1) * m + 2] if p < 2 else np.zeros((2, n))
            down = mine[p * m - 1 : p * m] if p > 0 else np.zeros((1, n))
            parts.append((up, down, own[:2], own[-1:]))
        places.append(parts)
    return places


def ends(rows, strip):
    return np.concatenate([rows[:, :strip], rows[:, -strip:]], 1)


def parts_of(table):
    high = np.asarray(jnp.asarray(table, jnp.bfloat16), np.float32)
    return high, table - high


def tables():
    places = edge_parts(256)
    row_table = np.zeros((3, 32, 2 * ROW_STRIP), np.float32)
    col_table = np.zeros((3, 8 * LEVELS, 2 * COL_STRIP), np.float32)
    for p, parts in enumerate(places):
        for k, (up, down, first, last) in enumerate(parts):
            row_table[p, 2 * k : 2 * k + 2] = ends(up, ROW_STRIP)
            row_table[p, 8 + k] = ends(down, ROW_STRIP)[0]
            row_table[p, 16 + 2 * k : 18 + 2 * k] = ends(first, ROW_STRIP)
            row_table[p, 24 + k] = ends(last, ROW_STRIP)[0]
            col_table[p, 8 * k : 8 * k + 6] = ends(np.concatenate([up, first, last, down]), COL_STRIP)
    high, low = parts_of(row_table)
    row_table = np.concatenate([high, high, low], 2)
    high, low = parts_of(col_table)
    none = np.zeros_like(low)
    col_table = np.concatenate(
        [np.concatenate([high, high], 2), np.concatenate([low, none], 2)], 1
    )
    return row_table, col_table


def split(a):
    high = a.astype(jnp.bfloat16)
    return high, (a - high.astype(jnp.float32)).astype(jnp.bfloat16)


dot = functools.partial(jnp.dot, preferred_element_type=jnp.float32)


def dot_split(a, weights):
    high, low = split(a)
    return dot(high, weights) + dot(low, weights)


def place(index, count):
    return jnp.where(index == 0, 0, jnp.where(index == count - 1, 2, 1))


def pyramid_kernel(
    rows_n, cols_n, x_hbm, rt_hbm, ct_hbm, c1_hbm, c12_hbm, c3_hbm, c4_hbm,
    o1, o2, o3, o4,
    strip, x, y1, y2, y3, y4, s1, s234, edge, rt, ct, c1, c12, c3, c4,
    zsend_up, zsend_down, zown, zfrom_low, zfrom_high,
    esend_up, esend_down, efrom_low, efrom_high,
    vsend, vfrom_low, vfrom_high,
    s_sem, x_sem, t_sem, e_sem, z_sem, v_sem,
):
    bands, height, width = x_hbm.shape
    tiles = width // 128
    r, c = lax.axis_index("row"), lax.axis_index("col")
    has_low_row, has_high_row = r > 0, r < rows_n - 1
    has_low_col, has_high_col = c > 0, c < cols_n - 1
    ys = (y1, y2, y3, y4)
    fields = (x,) + ys
    sizes = [height >> (k + 1) for k in range(LEVELS)]
    starts = [height - (height >> k) for k in range(LEVELS)]

    barrier = pltpu.get_barrier_semaphore()
    for axis, has, step in (
        ("row", has_low_row, -1), ("row", has_high_row, 1), ("col", has_low_col, -1), ("col", has_high_col, 1)
    ):

        @pl.when(has)
        def _(axis=axis, step=step):
            pl.semaphore_signal(
                barrier, inc=1, device_id={axis: lax.axis_index(axis) + step}, device_id_type=MESH
            )

    def load(source, target, sem):
        copy = pltpu.make_async_copy(source, target, sem)
        copy.start()
        return copy

    first_loads = [load(rt_hbm.at[place(r, rows_n)], rt, t_sem.at[0])]
    for b in range(bands):
        for e, begin in enumerate((0, height - ROW_STRIP)):
            first_loads.append(
                load(
                    x_hbm.at[b, begin : begin + ROW_STRIP],
                    strip.at[b, e * ROW_STRIP : (e + 1) * ROW_STRIP],
                    s_sem.at[e, b],
                )
            )
    band_loads = [
        [
            load(x_hbm.at[b, :, 128 * i : 128 * i + 128], x.at[b, i, PAD : PAD + height], x_sem.at[b, i])
            for i in range(tiles)
        ]
        for b in range(bands)
    ]
    rest = [
        load(ct_hbm.at[place(c, cols_n)], ct, t_sem.at[1]),
        load(c1_hbm, c1, t_sem.at[2]),
        load(c12_hbm, c12, t_sem.at[3]),
        load(c3_hbm, c3, t_sem.at[4]),
        load(c4_hbm, c4, t_sem.at[5]),
    ]

    for field in fields[:LEVELS]:
        size = field.shape[2] - 2 * PAD
        zeros = jnp.zeros((bands, tiles, PAD, 128), jnp.float32)
        field[:, :, 0:PAD] = zeros
        field[:, :, PAD + size :] = zeros

    lower_half = lax.broadcasted_iota(jnp.int32, (1, 128), 1) < 64

    def both_edges(a):
        return jnp.where(lower_half, a[:, :128], a[:, width - 128 :])

    for copy in first_loads:
        copy.wait()
    for b in range(bands):
        high, low = split(strip[b])
        z = dot(rt[...], jnp.concatenate([high, low, high], 0))
        zsend_up[b] = z[0:8]
        zsend_down[b] = z[8:16]
        zown[b] = z[16:32]
        esend_up[b] = both_edges(z[0:8])
        esend_down[b] = both_edges(z[8:16])

    neighbours = (
        has_low_row.astype(jnp.int32)
        + has_high_row.astype(jnp.int32)
        + has_low_col.astype(jnp.int32)
        + has_high_col.astype(jnp.int32)
    )
    pl.semaphore_wait(barrier, neighbours)

    def exchange(axis, has_low, has_high, up, down, from_low, from_high, sem):
        here = lax.axis_index(axis)
        to_high = pltpu.make_async_remote_copy(
            up, from_low, sem.at[0], sem.at[1], device_id={axis: here + 1}, device_id_type=MESH
        )
        to_low = pltpu.make_async_remote_copy(
            down, from_high, sem.at[2], sem.at[3], device_id={axis: here - 1}, device_id_type=MESH
        )
        pl.when(has_high)(to_high.start)
        pl.when(has_low)(to_low.start)

        def arrive():
            pl.when(has_low)(to_high.wait_recv)
            pl.when(has_high)(to_low.wait_recv)

        def sent():
            pl.when(has_high)(to_high.wait_send)
            pl.when(has_low)(to_low.wait_send)

        return arrive, sent

    e_arrive, e_sent = exchange(
        "row", has_low_row, has_high_row, esend_up, esend_down, efrom_low, efrom_high, e_sem
    )
    z_arrive, z_sent = exchange(
        "row", has_low_row, has_high_row, zsend_up, zsend_down, zfrom_low, zfrom_high, z_sem
    )

    for b in range(bands):
        for copy in band_loads[b]:
            copy.wait()

        def reduce_tile(i, carry, b=b):
            for source, target in zip(fields[:LEVELS], ys):
                size = target.shape[2] - 2 * PAD
                tap = [source[b, i, pl.ds(PAD - 2 + t, size, stride=2)] for t in range(5)]
                target[b, i, PAD : PAD + size] = (
                    0.0625 * (tap[0] + tap[4]) + 0.25 * (tap[1] + tap[3]) + 0.375 * tap[2]
                )
            return carry

        lax.fori_loop(0, tiles, reduce_tile, 0, unroll=UNROLL)

    for copy in rest:
        copy.wait()
    for b in range(bands):
        for k, y in enumerate(ys):
            edge[b, starts[k] : starts[k] + sizes[k]] = jnp.where(
                lower_half, y[b, 0, PAD : PAD + sizes[k]], y[b, tiles - 1, PAD : PAD + sizes[k]]
            )
        edge[b, starts[LEVELS - 1] + sizes[LEVELS - 1] :] = jnp.zeros((sizes[LEVELS - 1], 128), jnp.float32)
    e_arrive()
    lane = lax.broadcasted_iota(jnp.int32, (8, height), 1)
    for b in range(bands):
        first = jnp.where(has_low_row, efrom_low[b], 0.0) + both_edges(zown[b, 0:8])
        last = jnp.where(has_high_row, efrom_high[b], 0.0) + both_edges(zown[b, 8:16])
        for k in range(LEVELS):
            begin, end = starts[k], starts[k] + sizes[k]
            edge[b, begin : begin + 2] = edge[b, begin : begin + 2] + first[2 * k : 2 * k + 2]
            edge[b, end - 1 : end] = edge[b, end - 1 : end] + last[k : k + 1]
        high, low = split(edge[b])
        v = lax.dot_general(
            ct[...],
            jnp.concatenate([high, low], 1),
            (((1,), (1,)), ((), ())),
            preferred_element_type=jnp.float32,
        )
        v = v[: 8 * LEVELS] + v[8 * LEVELS :]
        picked = v[8 * LEVELS - 8 :]
        for k in range(LEVELS - 2, -1, -1):
            picked = jnp.where(lane < starts[k + 1], v[8 * k : 8 * k + 8], picked)
        vsend[b] = picked
    v_arrive, v_sent = exchange(
        "col", has_low_col, has_high_col, vsend, vsend, vfrom_low, vfrom_high, v_sem
    )

    z_arrive()
    for b in range(bands):
        first = jnp.where(has_low_row, zfrom_low[b], 0.0) + zown[b, 0:8]
        last = jnp.where(has_high_row, zfrom_high[b], 0.0) + zown[b, 8:16]
        for k, y in enumerate(ys):
            for i in range(tiles):
                lanes = slice(128 * i, 128 * i + 128)
                y[b, i, PAD : PAD + 2] = y[b, i, PAD : PAD + 2] + first[2 * k : 2 * k + 2, lanes]
                end = slice(PAD + sizes[k] - 1, PAD + sizes[k])
                y[b, i, end] = y[b, i, end] + last[k : k + 1, lanes]

    rows = sum(sizes[1:]) * bands
    base = 0
    for k in range(1, LEVELS):
        for b in range(bands):
            for i in range(tiles):
                high, low = split(ys[k][b, i, PAD : PAD + sizes[k]])
                s234[base : base + sizes[k], 128 * i : 128 * i + 128] = high
                s234[rows + base : rows + base + sizes[k], 128 * i : 128 * i + 128] = low
            base += sizes[k]
    half = width // 2
    near = lax.broadcasted_iota(jnp.int32, (1, 128), 1)
    for b in range(bands):
        for i in range(tiles):
            high, low = split(y1[b, i, PAD : PAD + sizes[0]])
            h, lanes = divmod(128 * i, half)
            s1[2 * h * sizes[0] : (2 * h + 1) * sizes[0], lanes : lanes + 128] = high
            s1[(2 * h + 1) * sizes[0] : (2 * h + 2) * sizes[0], lanes : lanes + 128] = low
        one = dot(s1[...], c1[...])
        for h in range(2):
            o1[b, :, half // 2 * h : half // 2 * (h + 1)] = (
                one[2 * h * sizes[0] : (2 * h + 1) * sizes[0]]
                + one[(2 * h + 1) * sizes[0] : (2 * h + 2) * sizes[0]]
            )
        left = y1[b, tiles // 2 - 1, PAD : PAD + sizes[0]]
        right = y1[b, tiles // 2, PAD : PAD + sizes[0]]
        middle = half // 2
        o1[b, :, middle - 128 : middle] = o1[b, :, middle - 128 : middle] + jnp.where(
            near == 127, 0.0625 * pltpu.roll(right, 127, 1), 0.0
        )
        o1[b, :, middle : middle + 128] = o1[b, :, middle : middle + 128] + jnp.where(
            near == 0, 0.0625 * pltpu.roll(left, 2, 1) + 0.25 * pltpu.roll(left, 1, 1), 0.0
        )
    two = dot(s234[...], c12[...])
    two = two[:rows] + two[rows:]
    three = dot_split(two[bands * sizes[1] :], c3[...])
    four = dot_split(three[bands * sizes[2] :], c4[...])
    for b in range(bands):
        o2[b] = two[b * sizes[1] : (b + 1) * sizes[1]]
        o3[b] = three[b * sizes[2] : (b + 1) * sizes[2]]
        o4[b] = four[b * sizes[3] : (b + 1) * sizes[3], : width >> 4]

    v_arrive()
    at = lax.broadcasted_iota(jnp.int32, (128, 128), 1)
    row = lax.broadcasted_iota(jnp.int32, (8, height), 0)
    for b in range(bands):
        own = vsend[b]
        first = jnp.where(has_low_col, vfrom_low[b], 0.0) + pltpu.roll(own, 6, 0)
        last = jnp.where(has_high_col, pltpu.roll(vfrom_high[b], 2, 0), 0.0) + pltpu.roll(own, 3, 0)
        cells = jnp.where(row < 2, first, jnp.where(row == 7, last, 0.0))
        for part, levels in ((0, (0,)), (1, (1, 2, 3))):
            square = jnp.concatenate(
                [cells[:, 128 * part : 128 * part + 128], jnp.zeros((120, 128), jnp.float32)], 0
            ).T
            for k in levels:
                out = (o1, o2, o3, o4)[k]
                begin = starts[k] - 128 * part
                value = square[begin : begin + sizes[k]]
                tile = min(out.shape[2], 128)
                mark = at[: sizes[k]]
                low_cells = jnp.where(mark < 2, value, 0.0)[:, :tile]
                high_cells = jnp.where(mark == tile - 1, pltpu.roll(value, tile - 8, 1), 0.0)[:, :tile]
                out[b, :, 0:tile] = out[b, :, 0:tile] + low_cells
                out[b, :, out.shape[2] - tile :] = out[b, :, out.shape[2] - tile :] + high_cells
    e_sent()
    z_sent()
    v_sent()


def store_kernel(*refs):
    sources, targets, sem = refs[:LEVELS], refs[LEVELS : 2 * LEVELS], refs[2 * LEVELS]
    copies = [pltpu.make_async_copy(s, t, sem.at[k]) for k, (s, t) in enumerate(zip(sources, targets))]
    for copy in copies:
        copy.start()
    for copy in copies:
        copy.wait()


def solution(mesh):
    rows_n, cols_n = mesh.shape["row"], mesh.shape["col"]
    row_table, col_table = tables()

    def local(relief):
        bands, height, width = relief.shape
        f32, bf16 = jnp.float32, jnp.bfloat16
        c1 = reduce_matrix(width // 2, False).T
        c12 = chain(width, False)[1].T
        c3 = reduce_matrix(width // 4, False).T
        c4 = np.zeros((width // 8, 128))
        c4[:, : width // 16] = reduce_matrix(width // 8, False).T
        consts = [jnp.asarray(a, bf16) for a in (row_table, col_table, c1, c12, c3, c4)]
        shapes = [(bands, height >> k, width >> k) for k in range(1, LEVELS + 1)]

        vmem = lambda *shape, dtype=f32: pltpu.VMEM(shape, dtype)
        scratch = [vmem(bands, 2 * ROW_STRIP, width)]
        scratch += [vmem(bands, width // 128, (height >> k) + 2 * PAD, 128) for k in range(LEVELS + 1)]
        rest = sum(height >> k for k in range(2, LEVELS + 1))
        scratch += [
            vmem(2 * height, width // 2, dtype=bf16), vmem(2 * bands * rest, width, dtype=bf16),
            vmem(bands, height, 128),
        ]
        scratch += [vmem(*a.shape, dtype=bf16) for a in (row_table[0], col_table[0], c1, c12, c3, c4)]
        scratch += [vmem(bands, n, width) for n in (8, 8, 16, 8, 8)]
        scratch += [vmem(bands, 8, 128)] * 4
        scratch += [vmem(bands, 8, height)] * 3
        scratch += [
            pltpu.SemaphoreType.DMA(n) for n in ((2, bands), (bands, width // 128), (6,), (4,), (4,), (4,))
        ]
        held = pl.pallas_call(
            functools.partial(pyramid_kernel, rows_n, cols_n),
            out_shape=[jax.ShapeDtypeStruct(s, f32) for s in shapes],
            in_specs=[pl.BlockSpec(memory_space=pltpu.HBM)] * 7,
            out_specs=[pl.BlockSpec(memory_space=pltpu.VMEM)] * LEVELS,
            scratch_shapes=scratch,
            compiler_params=pltpu.CompilerParams(
                collective_id=0, has_side_effects=True, vmem_limit_bytes=40 << 20
            ),
            name="pyramid",
        )(*[pltpu.with_memory_space_constraint(a, pltpu.HBM) for a in (relief, *consts)])
        return pl.pallas_call(
            store_kernel,
            out_shape=[jax.ShapeDtypeStruct(s, f32) for s in shapes],
            in_specs=[pl.BlockSpec(memory_space=pltpu.VMEM)] * LEVELS,
            out_specs=[pl.BlockSpec(memory_space=pltpu.HBM)] * LEVELS,
            scratch_shapes=[pltpu.SemaphoreType.DMA((LEVELS,))],
            compiler_params=pltpu.CompilerParams(vmem_limit_bytes=16 << 20),
            name="store",
        )(*held)

    spec = P(None, "row", "col")
    return jax.shard_map(local, mesh=mesh, in_specs=(spec,), out_specs=(spec,) * LEVELS, check_vma=False)
```

```python
import functools

import jax
import jax.numpy as jnp
import numpy as np
from jax import lax
from jax.experimental import pallas as pl
from jax.experimental.pallas import tpu as pltpu
from jax.sharding import PartitionSpec as P

MESH = pl.DeviceIdType.MESH
BINOMIAL = np.array([1, 4, 6, 4, 1]) / 16
LEVELS = 4
PAD = 8
ROW_STRIP = 32
COL_STRIP = 64
UNROLL = 4


def reduce_matrix(n, reflect):
    d = np.zeros((n // 2, n))
    for i in range(n // 2):
        for t in range(5):
            c = 2 * i - 2 + t
            if c < 0 or c >= n:
                if not reflect:
                    continue
                c = -c if c < 0 else 2 * (n - 1) - c
            d[i, c] += BINOMIAL[t]
    return d


def chain(n, reflect):
    out, m = [], np.eye(n)
    for _ in range(LEVELS):
        m = reduce_matrix(m.shape[0], reflect) @ m
        out.append(m)
    return out


def edge_parts(n):
    whole, alone = chain(3 * n, True), chain(n, False)
    places = []
    for p in range(3):
        parts = []
        for k in range(LEVELS):
            m = n >> (k + 1)
            mine = whole[k][:, p * n : (p + 1) * n]
            own = mine[p * m : (p + 1) * m] - alone[k]
            assert not own[2:-1].any()
            up = mine[(p + 1) * m : (p + 1) * m + 2] if p < 2 else np.zeros((2, n))
            down = mine[p * m - 1 : p * m] if p > 0 else np.zeros((1, n))
            parts.append((up, down, own[:2], own[-1:]))
        places.append(parts)
    return places


def ends(rows, strip):
    return np.concatenate([rows[:, :strip], rows[:, -strip:]], 1)


def parts_of(table):
    high = np.asarray(jnp.asarray(table, jnp.bfloat16), np.float32)
    return high, table - high


def tables():
    places = edge_parts(256)
    row_table = np.zeros((3, 32, 2 * ROW_STRIP), np.float32)
    col_table = np.zeros((3, 8 * LEVELS, 2 * COL_STRIP), np.float32)
    for p, parts in enumerate(places):
        for k, (up, down, first, last) in enumerate(parts):
            row_table[p, 2 * k : 2 * k + 2] = ends(up, ROW_STRIP)
            row_table[p, 8 + 2 * k] = ends(down, ROW_STRIP)[0]
            row_table[p, 16 + 2 * k : 18 + 2 * k] = ends(first, ROW_STRIP)
            row_table[p, 24 + 2 * k] = ends(last, ROW_STRIP)[0]
            col_table[p, 8 * k : 8 * k + 6] = ends(np.concatenate([up, first, last, down]), COL_STRIP)
    high, low = parts_of(row_table)
    row_table = np.concatenate([high, high, low], 2)
    high, low = parts_of(col_table)
    none = np.zeros_like(low)
    col_table = np.concatenate(
        [np.concatenate([high, high], 2), np.concatenate([low, none], 2)], 1
    )
    return row_table, col_table


ABOVE = ((0, 1), (2, 3), (4, 5), (6, 7))
BELOW = (8, 10, 12, 14)


def whole_rows(n):
    whole = chain(3 * n, True)
    table = np.zeros((3, n, n + 128), np.float32)
    for p in range(3):
        for k in range(LEVELS):
            m, begin = n >> (k + 1), n - (n >> k)
            mine = whole[k][:, p * n : (p + 1) * n]
            table[p, :, begin : begin + m] = mine[p * m : (p + 1) * m].T
            if p < 2:
                for lane, cells in zip(ABOVE[k], mine[(p + 1) * m :]):
                    table[p, :, n + lane] = cells
            if p > 0:
                table[p, :, n + BELOW[k]] = mine[p * m - 1]
    return np.stack(parts_of(table), 1)


def split(a):
    high = a.astype(jnp.bfloat16)
    return high, (a - high.astype(jnp.float32)).astype(jnp.bfloat16)


dot = functools.partial(jnp.dot, preferred_element_type=jnp.float32)


def dot_split(a, weights):
    high, low = split(a)
    return dot(high, weights) + dot(low, weights)


def place(index, count):
    return jnp.where(index == 0, 0, jnp.where(index == count - 1, 2, 1))


def pyramid_kernel(
    rows_n, cols_n, x_hbm, rt_hbm, ct_hbm, wr_hbm, c1_hbm, c12_hbm, c3_hbm, c4_hbm,
    o1, o2, o3, o4, low_rows, high_rows, corners,
    strip, x, y1, y2, y3, y4, s1, s234, rt, ct, wr, c1, c12, c3, c4, zown,
    zsend_up, zsend_down, zfrom_low, zfrom_high,
    esend, efrom_low, efrom_high,
    vown, vsend_up, vsend_down, vfrom_low, vfrom_high,
    s_sem, x_sem, t_sem, e_sem, z_sem, v_sem, told,
):
    bands, height, width = x_hbm.shape
    tiles = width // 128
    r, c = lax.axis_index("row"), lax.axis_index("col")
    has_low_row, has_high_row = r > 0, r < rows_n - 1
    has_low_col, has_high_col = c > 0, c < cols_n - 1
    ys = (y1, y2, y3, y4)
    fields = (x,) + ys
    sizes = [height >> (k + 1) for k in range(LEVELS)]
    starts = [height - (height >> k) for k in range(LEVELS)]

    place_in_line = r % 8
    far_high = (place_in_line == 7) & has_high_row
    far_low = (place_in_line == 0) & has_low_row
    hears_high = (place_in_line == 6) & (r + 2 < rows_n)
    hears_low = (place_in_line == 1) & (r > 1)
    barrier = pltpu.get_barrier_semaphore()
    for axis, has, step in (
        ("row", has_low_row & jnp.logical_not(far_low), -1), ("row", has_high_row & jnp.logical_not(far_high), 1),
        ("row", far_low, -2), ("row", far_high, 2),
        ("col", has_low_col, -1), ("col", has_high_col, 1),
    ):

        @pl.when(has)
        def _(axis=axis, step=step):
            pl.semaphore_signal(
                barrier, inc=1, device_id={axis: lax.axis_index(axis) + step}, device_id_type=MESH
            )

    def load(source, target, sem):
        copy = pltpu.make_async_copy(source, target, sem)
        copy.start()
        return copy

    def load_tile(b, i):
        return load(x_hbm.at[b, :, 128 * i : 128 * i + 128], x.at[b, i, PAD : PAD + height], x_sem.at[b, i])

    col_loads = [load(ct_hbm.at[place(c, cols_n)], ct, t_sem.at[0])]
    for b in range(bands):
        col_loads += [load_tile(b, 0), load_tile(b, tiles - 1)]
    col_loads.append(load(wr_hbm.at[place(r, rows_n)], wr, t_sem.at[1]))
    row_loads = [load(rt_hbm.at[place(r, rows_n)], rt, t_sem.at[2])]
    for b in range(bands):
        for e, begin in enumerate((0, height - ROW_STRIP)):
            row_loads.append(
                load(
                    x_hbm.at[b, begin : begin + ROW_STRIP],
                    strip.at[b, e * ROW_STRIP : (e + 1) * ROW_STRIP],
                    s_sem.at[e, b],
                )
            )
    row_loads += [
        load(source, target, t_sem.at[3 + n])
        for n, (source, target) in enumerate(((c1_hbm, c1), (c12_hbm, c12), (c3_hbm, c3), (c4_hbm, c4)))
    ]
    band_loads = [[load_tile(b, i) for i in range(1, tiles - 1)] for b in range(bands)]

    for field in fields[:LEVELS]:
        size = field.shape[2] - 2 * PAD
        zeros = jnp.zeros((bands, tiles, PAD, 128), jnp.float32)
        field[:, :, 0:PAD] = zeros
        field[:, :, PAD + size :] = zeros

    lower_half = lax.broadcasted_iota(jnp.int32, (1, 128), 1) < 64
    for copy in col_loads:
        copy.wait()
    raw = []
    for b in range(bands):
        high, low = split(
            jnp.where(lower_half, x[b, 0, PAD : PAD + height], x[b, tiles - 1, PAD : PAD + height])
        )
        v = lax.dot_general(
            ct[...],
            jnp.concatenate([high, low], 1),
            (((1,), (1,)), ((), ())),
            preferred_element_type=jnp.float32,
        )
        raw.append(v[: 8 * LEVELS] + v[8 * LEVELS :])
    raw = jnp.concatenate(raw, 0)
    high, low = split(raw)
    v = dot(jnp.concatenate([high, low], 0), wr[0])
    v = v[: raw.shape[0]] + v[raw.shape[0] :] + dot(high, wr[1])
    lane = lax.broadcasted_iota(jnp.int32, (8, height + 128), 1)
    row = lax.broadcasted_iota(jnp.int32, (8, height + 128), 0)
    beyond = lane - height
    level_of = jnp.where(
        lane < height,
        sum((lane >= start).astype(jnp.int32) for start in starts[1:]),
        (beyond & 7) >> 1,
    )
    up, down = jnp.zeros(lane.shape, jnp.float32), jnp.zeros(lane.shape, jnp.float32)
    for b in range(bands):
        begin = 8 * LEVELS * b
        picked = v[begin : begin + 8]
        for k in range(1, LEVELS):
            picked = jnp.where(level_of == k, v[begin + 8 * k : begin + 8 * k + 8], picked)
        vown[b] = picked
        up = jnp.where((row >= 2 * b) & (row < 2 * b + 2), pltpu.roll(picked, 2 * b, 0), up)
        down = jnp.where(row == b, pltpu.roll(picked, b + 3, 0), down)
    vsend_up[...] = up
    vsend_down[...] = down

    expected = (
        (has_low_row & jnp.logical_not(far_low), has_high_row & jnp.logical_not(far_high))
        + (hears_low, hears_high, has_low_col, has_high_col)
    )
    pl.semaphore_wait(barrier, sum(has.astype(jnp.int32) for has in expected))
    for has, step in ((hears_high, 1), (hears_low, -1)):

        @pl.when(has)
        def _(step=step):
            pl.semaphore_signal(
                told, inc=1, device_id={"row": lax.axis_index("row") + step}, device_id_type=MESH
            )

    def exchange(axis, has_low, has_high, up, down, from_low, from_high, sem):
        here = lax.axis_index(axis)
        to_high = pltpu.make_async_remote_copy(
            up, from_low, sem.at[0], sem.at[1], device_id={axis: here + 1}, device_id_type=MESH
        )
        to_low = pltpu.make_async_remote_copy(
            down, from_high, sem.at[2], sem.at[3], device_id={axis: here - 1}, device_id_type=MESH
        )
        pl.when(has_high)(to_high.start)
        pl.when(has_low)(to_low.start)

        def arrive():
            pl.when(has_low)(to_high.wait_recv)
            pl.when(has_high)(to_low.wait_recv)

        def sent():
            pl.when(has_high)(to_high.wait_send)
            pl.when(has_low)(to_low.wait_send)

        return arrive, sent

    v_arrive, v_sent = exchange(
        "col", has_low_col, has_high_col, vsend_up, vsend_down, vfrom_low, vfrom_high, v_sem
    )

    half = width // 2
    near = lax.broadcasted_iota(jnp.int32, (1, 128), 1)

    def across_middle(out, left, right):
        before = out[0][:, half // 2 - 128 :] + jnp.where(near == 127, 0.0625 * pltpu.roll(right, 127, 1), 0.0)
        after = out[1][:, :128] + jnp.where(
            near == 0, 0.0625 * pltpu.roll(left, 2, 1) + 0.25 * pltpu.roll(left, 1, 1), 0.0
        )
        return jnp.concatenate([out[0][:, : half // 2 - 128], before], 1), jnp.concatenate(
            [after, out[1][:, 128:]], 1
        )

    for copy in row_loads:
        copy.wait()
    spilled = []
    for b in range(bands):
        high, low = split(strip[b])
        z = dot(rt[...], jnp.concatenate([high, low, high], 0))
        zown[b] = z[16:32]
        spilled.append(z[0:16])
    spilled = jnp.concatenate(spilled, 0)
    count = spilled.shape[0]
    high, low = split(spilled)
    one = dot(
        jnp.concatenate([high[:, :half], low[:, :half], high[:, half:], low[:, half:]], 0), c1[...]
    )
    one = across_middle(
        (one[:count] + one[count : 2 * count], one[2 * count : 3 * count] + one[3 * count :]),
        spilled[:, half - 128 : half],
        spilled[:, half : half + 128],
    )
    two = dot(jnp.concatenate([high, low], 0), c12[...])
    two = two[:count] + two[count:]
    three = dot_split(two, c3[...])
    four = dot_split(three, c4[...])
    for b in range(bands):
        for side, target in enumerate((zsend_up, zsend_down)):
            g = slice(16 * b + 8 * side, 16 * b + 8 * side + 8)
            pad = jnp.zeros((8, width // 4 - 128), jnp.float32)
            group = lax.broadcasted_iota(jnp.int32, (8, width // 4), 0)
            packed = jnp.where(group < 6, jnp.concatenate([three[g], pad], 1), jnp.concatenate([four[g], pad], 1))
            packed = jnp.where(group < 4, two[g], packed)
            packed = jnp.where(group == 1, pltpu.roll(one[1][g], 1, 0), packed)
            target[b] = jnp.where(group == 0, one[0][g], packed)
    pl.when(far_high | far_low)(lambda: pl.semaphore_wait(told, 1))
    z_arrive, z_sent = exchange(
        "row", has_low_row, has_high_row, zsend_up, zsend_down, zfrom_low, zfrom_high, z_sem
    )

    for b in range(bands):
        for copy in band_loads[b]:
            copy.wait()

        def reduce_tile(i, carry, b=b):
            for source, target in zip(fields[:LEVELS], ys):
                size = target.shape[2] - 2 * PAD
                tap = [source[b, i, pl.ds(PAD - 2 + t, size, stride=2)] for t in range(5)]
                target[b, i, PAD : PAD + size] = (
                    0.0625 * (tap[0] + tap[4]) + 0.25 * (tap[1] + tap[3]) + 0.375 * tap[2]
                )
            return carry

        lax.fori_loop(0, tiles, reduce_tile, 0, unroll=UNROLL)

    v_arrive()
    for b in range(bands):
        own = vown[b]
        low = jnp.where(has_low_col, vfrom_low[...], 0.0)
        high = jnp.where(has_high_col, vfrom_high[...], 0.0)
        first = pltpu.roll(own, 6, 0) + pltpu.roll(low, (8 - 2 * b) % 8, 0)
        last = pltpu.roll(own, 3, 0) + pltpu.roll(high, 7 - b, 0)
        both = jnp.where(row < 2, first, jnp.where(row == 7, last, 0.0))
        vown[b] = both
        esend[b] = both[:, height:]
    e_arrive, e_sent = exchange(
        "row", has_low_row, has_high_row, esend, esend, efrom_low, efrom_high, e_sem
    )

    for b in range(bands):
        for k, y in enumerate(ys):
            for i in range(tiles):
                lanes = slice(128 * i, 128 * i + 128)
                y[b, i, PAD : PAD + 2] = y[b, i, PAD : PAD + 2] + zown[b, 2 * k : 2 * k + 2, lanes]
                end = slice(PAD + sizes[k] - 1, PAD + sizes[k])
                y[b, i, end] = y[b, i, end] + zown[b, 8 + 2 * k : 9 + 2 * k, lanes]

    rows = sum(sizes[1:]) * bands
    base = 0
    for k in range(1, LEVELS):
        for b in range(bands):
            for i in range(tiles):
                high, low = split(ys[k][b, i, PAD : PAD + sizes[k]])
                s234[base : base + sizes[k], 128 * i : 128 * i + 128] = high
                s234[rows + base : rows + base + sizes[k], 128 * i : 128 * i + 128] = low
            base += sizes[k]
    for b in range(bands):
        for i in range(tiles):
            high, low = split(y1[b, i, PAD : PAD + sizes[0]])
            h, lanes = divmod(128 * i, half)
            s1[2 * h * sizes[0] : (2 * h + 1) * sizes[0], lanes : lanes + 128] = high
            s1[(2 * h + 1) * sizes[0] : (2 * h + 2) * sizes[0], lanes : lanes + 128] = low
        one = dot(s1[...], c1[...])
        size = sizes[0]
        one = across_middle(
            (one[:size] + one[size : 2 * size], one[2 * size : 3 * size] + one[3 * size :]),
            y1[b, tiles // 2 - 1, PAD : PAD + size],
            y1[b, tiles // 2, PAD : PAD + size],
        )
        o1[b, :, : half // 2] = one[0]
        o1[b, :, half // 2 :] = one[1]
    two = dot(s234[...], c12[...])
    two = two[:rows] + two[rows:]
    three = dot_split(two[bands * sizes[1] :], c3[...])
    four = dot_split(three[bands * sizes[2] :], c4[...])
    for b in range(bands):
        o2[b] = two[b * sizes[1] : (b + 1) * sizes[1]]
        o3[b] = three[b * sizes[2] : (b + 1) * sizes[2]]
        o4[b] = four[b * sizes[3] : (b + 1) * sizes[3], : width >> 4]

    at = lax.broadcasted_iota(jnp.int32, (128, 128), 1)
    for b in range(bands):
        for part, levels in ((0, (0,)), (1, (1, 2, 3))):
            square = jnp.concatenate(
                [vown[b, :, 128 * part : 128 * part + 128], jnp.zeros((120, 128), jnp.float32)], 0
            ).T
            for k in levels:
                out = (o1, o2, o3, o4)[k]
                begin = starts[k] - 128 * part
                value = square[begin : begin + sizes[k]]
                tile = min(out.shape[2], 128)
                mark = at[: sizes[k]]
                low_cells = jnp.where(mark < 2, value, 0.0)[:, :tile]
                high_cells = jnp.where(mark == tile - 1, pltpu.roll(value, tile - 8, 1), 0.0)[:, :tile]
                out[b, :, 0:tile] = out[b, :, 0:tile] + low_cells
                out[b, :, out.shape[2] - tile :] = out[b, :, out.shape[2] - tile :] + high_cells

    above = lax.broadcasted_iota(jnp.int32, (8, 128), 1) < 8
    z_arrive()
    for b in range(bands):
        low_rows[b] = jnp.where(has_low_row, zfrom_low[b], 0.0)
        high_rows[b] = jnp.where(has_high_row, zfrom_high[b], 0.0)
    e_arrive()
    for b in range(bands):
        corners[b] = jnp.where(
            above,
            jnp.where(has_low_row, efrom_low[b], 0.0),
            jnp.where(has_high_row, efrom_high[b], 0.0),
        )
    e_sent()
    z_sent()
    v_sent()


def store_kernel(a1, a2, a3, a4, low_rows, high_rows, corners, o1, o2, o3, o4, t1, t2, t3, t4, in_sem, edge_sem):
    bands = a1.shape[0]
    copies = []
    for k, (source, target) in enumerate(((a1, o1), (a2, o2), (a3, o3))):
        inner = slice(8, source.shape[1] - 8)
        copies.append(pltpu.make_async_copy(source.at[:, inner], target.at[:, inner], in_sem.at[k]))
        copies[-1].start()
    lane = lax.broadcasted_iota(jnp.int32, (16, 128), 1)
    for b in range(bands):
        cells = jnp.concatenate([corners[b], jnp.zeros((120, 128), jnp.float32)], 0).T[:16]
        first = jnp.where(lane < 2, cells, 0.0)
        last = jnp.where(lane == 127, pltpu.roll(cells, 120, 1), 0.0)
        last_half = jnp.where(lane == 63, pltpu.roll(cells, 56, 1), 0.0)
        for side, rows in enumerate((low_rows[b], high_rows[b])):
            for k, (source, target) in enumerate(zip((a1, a2, a3, a4), (t1, t2, t3, t4))):
                size, wide = source.shape[1:]
                count = 2 if side == 0 and k > 0 else 1
                at = slice(8 * side + 2 * k, 8 * side + 2 * k + count)
                if k == 0:
                    none = jnp.zeros((1, wide - 256), jnp.float32)
                    more = jnp.concatenate([rows[0:1], rows[1:2]], 1)
                    more = more + jnp.concatenate([first[at], none, last[at]], 1)
                else:
                    more = rows[2 * k : 2 * k + count, :wide]
                    if k == 1:
                        more = more + jnp.concatenate([first[at], last[at]], 1)
                    elif k == 2:
                        more = more + first[at] + last[at]
                    else:
                        more = more + (first[at] + last_half[at])[:, :wide]
                still = jnp.zeros((8 - count, wide), jnp.float32)
                if side == 0:
                    target[side, b] = source[b, 0:8] + jnp.concatenate([more, still], 0)
                else:
                    target[side, b] = source[b, size - 8 : size] + jnp.concatenate([still, more], 0)
    for k, (source, target) in enumerate(((t1, o1), (t2, o2), (t3, o3), (t4, o4))):
        size = target.shape[1]
        for side, begin in enumerate((0, size - 8)):
            copies.append(
                pltpu.make_async_copy(source.at[side], target.at[:, begin : begin + 8], edge_sem.at[side, k])
            )
            copies[-1].start()
    for copy in copies:
        copy.wait()


def solution(mesh):
    rows_n, cols_n = mesh.shape["row"], mesh.shape["col"]
    row_table, col_table = tables()
    all_rows = whole_rows(256)

    def local(relief):
        bands, height, width = relief.shape
        f32, bf16 = jnp.float32, jnp.bfloat16
        c1 = reduce_matrix(width // 2, False).T
        c12 = chain(width, False)[1].T
        c3 = reduce_matrix(width // 4, False).T
        c4 = np.zeros((width // 8, 128))
        c4[:, : width // 16] = reduce_matrix(width // 8, False).T
        consts = [jnp.asarray(a, bf16) for a in (row_table, col_table, all_rows, c1, c12, c3, c4)]
        shapes = [(bands, height >> k, width >> k) for k in range(1, LEVELS + 1)]

        vmem = lambda *shape, dtype=f32: pltpu.VMEM(shape, dtype)
        scratch = [vmem(bands, 2 * ROW_STRIP, width)]
        scratch += [vmem(bands, width // 128, (height >> k) + 2 * PAD, 128) for k in range(LEVELS + 1)]
        rest = sum(height >> k for k in range(2, LEVELS + 1))
        scratch += [
            vmem(2 * height, width // 2, dtype=bf16), vmem(2 * bands * rest, width, dtype=bf16),
        ]
        scratch += [vmem(*a.shape, dtype=bf16) for a in (row_table[0], col_table[0], all_rows[0], c1, c12, c3, c4)]
        scratch += [vmem(bands, 16, width)]
        scratch += [vmem(bands, 8, width // 4)] * 4
        scratch += [vmem(bands, 8, 128)] * 3
        scratch += [vmem(bands, 8, height + 128)] + [vmem(8, height + 128)] * 4
        scratch += [
            pltpu.SemaphoreType.DMA(n) for n in ((2, bands), (bands, width // 128), (7,), (4,), (4,), (4,))
        ]
        scratch += [pltpu.SemaphoreType.REGULAR]
        extra = [(bands, 8, width // 4)] * 2 + [(bands, 8, 128)]
        held = pl.pallas_call(
            functools.partial(pyramid_kernel, rows_n, cols_n),
            out_shape=[jax.ShapeDtypeStruct(s, f32) for s in shapes + extra],
            in_specs=[pl.BlockSpec(memory_space=pltpu.HBM)] * 8,
            out_specs=[pl.BlockSpec(memory_space=pltpu.VMEM)] * (LEVELS + 3),
            scratch_shapes=scratch,
            compiler_params=pltpu.CompilerParams(
                collective_id=0, has_side_effects=True, vmem_limit_bytes=40 << 20
            ),
            name="pyramid",
        )(*[pltpu.with_memory_space_constraint(a, pltpu.HBM) for a in (relief, *consts)])
        return pl.pallas_call(
            store_kernel,
            out_shape=[jax.ShapeDtypeStruct(s, f32) for s in shapes],
            in_specs=[pl.BlockSpec(memory_space=pltpu.VMEM)] * (LEVELS + 3),
            out_specs=[pl.BlockSpec(memory_space=pltpu.HBM)] * LEVELS,
            scratch_shapes=[vmem(2, bands, 8, across) for _, _, across in shapes]
            + [pltpu.SemaphoreType.DMA((LEVELS - 1,)), pltpu.SemaphoreType.DMA((2, LEVELS))],
            compiler_params=pltpu.CompilerParams(vmem_limit_bytes=16 << 20),
            name="store",
        )(*held)

    spec = P(None, "row", "col")
    return jax.shard_map(local, mesh=mesh, in_specs=(spec,), out_specs=(spec,) * LEVELS, check_vma=False)
```

```python
import functools

import jax
import jax.numpy as jnp
import numpy as np
from jax import lax
from jax.experimental import pallas as pl
from jax.experimental.pallas import tpu as pltpu
from jax.sharding import PartitionSpec as P

MESH = pl.DeviceIdType.MESH
BINOMIAL = np.array([1, 4, 6, 4, 1]) / 16
LEVELS = 4
PAD = 8
ROW_STRIP = 32
COL_STRIP = 64
UNROLL = 2
EARLY = 1


def reduce_matrix(n, reflect):
    d = np.zeros((n // 2, n))
    for i in range(n // 2):
        for t in range(5):
            c = 2 * i - 2 + t
            if c < 0 or c >= n:
                if not reflect:
                    continue
                c = -c if c < 0 else 2 * (n - 1) - c
            d[i, c] += BINOMIAL[t]
    return d


def chain(n, reflect):
    out, m = [], np.eye(n)
    for _ in range(LEVELS):
        m = reduce_matrix(m.shape[0], reflect) @ m
        out.append(m)
    return out


def edge_parts(n):
    whole, alone = chain(3 * n, True), chain(n, False)
    places = []
    for p in range(3):
        parts = []
        for k in range(LEVELS):
            m = n >> (k + 1)
            mine = whole[k][:, p * n : (p + 1) * n]
            own = mine[p * m : (p + 1) * m] - alone[k]
            assert not own[2:-1].any()
            up = mine[(p + 1) * m : (p + 1) * m + 2] if p < 2 else np.zeros((2, n))
            down = mine[p * m - 1 : p * m] if p > 0 else np.zeros((1, n))
            parts.append((up, down, own[:2], own[-1:]))
        places.append(parts)
    return places


def ends(rows, strip):
    return np.concatenate([rows[:, :strip], rows[:, -strip:]], 1)


def parts_of(table):
    high = np.asarray(jnp.asarray(table, jnp.bfloat16), np.float32)
    return high, table - high


def tables():
    places = edge_parts(256)
    row_table = np.zeros((3, 32, 2 * ROW_STRIP), np.float32)
    col_table = np.zeros((3, 8 * LEVELS, 2 * COL_STRIP), np.float32)
    for p, parts in enumerate(places):
        for k, (up, down, first, last) in enumerate(parts):
            row_table[p, 2 * k : 2 * k + 2] = ends(up, ROW_STRIP)
            row_table[p, 8 + 2 * k] = ends(down, ROW_STRIP)[0]
            row_table[p, 16 + 2 * k : 18 + 2 * k] = ends(first, ROW_STRIP)
            row_table[p, 24 + 2 * k] = ends(last, ROW_STRIP)[0]
            col_table[p, 8 * k : 8 * k + 6] = ends(np.concatenate([up, first, last, down]), COL_STRIP)
    high, low = parts_of(row_table)
    row_table = np.concatenate([high, high, low], 2)
    high, low = parts_of(col_table)
    none = np.zeros_like(low)
    col_table = np.concatenate(
        [np.concatenate([high, high], 2), np.concatenate([low, none], 2)], 1
    )
    return row_table, col_table


ABOVE = ((0, 1), (2, 3), (4, 5), (6, 7))
BELOW = (8, 10, 12, 14)


def whole_rows(n):
    whole = chain(3 * n, True)
    table = np.zeros((3, n, n + 128), np.float32)
    for p in range(3):
        for k in range(LEVELS):
            m, begin = n >> (k + 1), n - (n >> k)
            mine = whole[k][:, p * n : (p + 1) * n]
            table[p, :, begin : begin + m] = mine[p * m : (p + 1) * m].T
            if p < 2:
                for lane, cells in zip(ABOVE[k], mine[(p + 1) * m :]):
                    table[p, :, n + lane] = cells
            if p > 0:
                table[p, :, n + BELOW[k]] = mine[p * m - 1]
    return np.stack(parts_of(table), 1)


def split(a):
    high = a.astype(jnp.bfloat16)
    return high, (a - high.astype(jnp.float32)).astype(jnp.bfloat16)


dot = functools.partial(jnp.dot, preferred_element_type=jnp.float32)


def dot_split(a, weights):
    high, low = split(a)
    return dot(high, weights) + dot(low, weights)


def place(index, count):
    return jnp.where(index == 0, 0, jnp.where(index == count - 1, 2, 1))


def pyramid_kernel(
    rows_n, cols_n, x_hbm, rt_hbm, ct_hbm, wr_hbm, c1_hbm, c12_hbm, c3_hbm, c4_hbm,
    o1, o2, o3, o4, low_rows, high_rows, corners,
    strip, x, y1, y2, y3, y4, s1, s234, rt, ct, wr, c1, c12, c3, c4, zown,
    zsend_up, zsend_down, zfrom_low, zfrom_high,
    esend, efrom_low, efrom_high,
    vown, vsend_up, vsend_down, vfrom_low, vfrom_high,
    s_sem, x_sem, t_sem, e_sem, z_sem, v_sem, told,
):
    bands, height, width = x_hbm.shape
    tiles = width // 128
    r, c = lax.axis_index("row"), lax.axis_index("col")
    has_low_row, has_high_row = r > 0, r < rows_n - 1
    has_low_col, has_high_col = c > 0, c < cols_n - 1
    ys = (y1, y2, y3, y4)
    fields = (x,) + ys
    sizes = [height >> (k + 1) for k in range(LEVELS)]
    starts = [height - (height >> k) for k in range(LEVELS)]

    place_in_line = r % 8
    far_high = (place_in_line == 7) & has_high_row
    far_low = (place_in_line == 0) & has_low_row
    hears_high = (place_in_line == 6) & (r + 2 < rows_n)
    hears_low = (place_in_line == 1) & (r > 1)
    barrier = pltpu.get_barrier_semaphore()
    for axis, has, step in (
        ("row", has_low_row & jnp.logical_not(far_low), -1), ("row", has_high_row & jnp.logical_not(far_high), 1),
        ("row", far_low, -2), ("row", far_high, 2),
        ("col", has_low_col, -1), ("col", has_high_col, 1),
    ):

        @pl.when(has)
        def _(axis=axis, step=step):
            pl.semaphore_signal(
                barrier, inc=1, device_id={axis: lax.axis_index(axis) + step}, device_id_type=MESH
            )

    def load(source, target, sem):
        copy = pltpu.make_async_copy(source, target, sem)
        copy.start()
        return copy

    def tile_copy(b, i):
        return pltpu.make_async_copy(
            x_hbm.at[b, :, 128 * i : 128 * i + 128], x.at[b, i, PAD : PAD + height], x_sem.at[b, i]
        )

    def load_tile(b, i):
        copy = tile_copy(b, i)
        copy.start()
        return copy

    col_loads = [load(ct_hbm.at[place(c, cols_n)], ct, t_sem.at[0])]
    for b in range(bands):
        col_loads += [load_tile(b, 0), load_tile(b, tiles - 1)]
    wr_load = load(wr_hbm.at[place(r, rows_n)], wr, t_sem.at[1])
    for field in fields[:LEVELS]:
        size = field.shape[2] - 2 * PAD
        zeros = jnp.zeros((bands, tiles, PAD, 128), jnp.float32)
        field[:, :, 0:PAD] = zeros
        field[:, :, PAD + size :] = zeros

    lower_half = lax.broadcasted_iota(jnp.int32, (1, 128), 1) < 64
    for copy in col_loads:
        copy.wait()
    row_loads = [load(rt_hbm.at[place(r, rows_n)], rt, t_sem.at[2])]
    for b in range(bands):
        for e, begin in enumerate((0, height - ROW_STRIP)):
            row_loads.append(
                load(
                    x_hbm.at[b, begin : begin + ROW_STRIP],
                    strip.at[b, e * ROW_STRIP : (e + 1) * ROW_STRIP],
                    s_sem.at[e, b],
                )
            )
    row_loads += [
        load(source, target, t_sem.at[3 + n])
        for n, (source, target) in enumerate(((c1_hbm, c1), (c12_hbm, c12), (c3_hbm, c3), (c4_hbm, c4)))
    ]
    for b in range(bands):
        for i in range(1, tiles - 1):
            tile_copy(b, i).start()
    parts = []
    for b in range(bands):
        parts.append(
            jnp.concatenate(
                split(
                    jnp.where(lower_half, x[b, 0, PAD : PAD + height], x[b, tiles - 1, PAD : PAD + height])
                ),
                1,
            )
        )
    v = lax.dot_general(
        ct[...],
        jnp.concatenate(parts, 0),
        (((1,), (1,)), ((), ())),
        preferred_element_type=jnp.float32,
    )
    v = v[: 8 * LEVELS] + v[8 * LEVELS :]
    raw = [v[:, b * height : (b + 1) * height] for b in range(bands)]
    raw = jnp.concatenate(raw, 0)
    wr_load.wait()
    high, low = split(raw)
    v = dot(jnp.concatenate([high, low], 0), wr[0])
    v = v[: raw.shape[0]] + v[raw.shape[0] :] + dot(high, wr[1])
    lane = lax.broadcasted_iota(jnp.int32, (8, height + 128), 1)
    row = lax.broadcasted_iota(jnp.int32, (8, height + 128), 0)
    beyond = lane - height
    level_of = jnp.where(
        lane < height,
        sum((lane >= start).astype(jnp.int32) for start in starts[1:]),
        (beyond & 7) >> 1,
    )
    up, down = jnp.zeros(lane.shape, jnp.float32), jnp.zeros(lane.shape, jnp.float32)
    for b in range(bands):
        begin = 8 * LEVELS * b
        picked = v[begin : begin + 8]
        for k in range(1, LEVELS):
            picked = jnp.where(level_of == k, v[begin + 8 * k : begin + 8 * k + 8], picked)
        vown[b] = picked
        up = jnp.where((row >= 2 * b) & (row < 2 * b + 2), pltpu.roll(picked, 2 * b, 0), up)
        down = jnp.where(row == b, pltpu.roll(picked, b + 3, 0), down)
    vsend_up[...] = up
    vsend_down[...] = down

    expected = (
        (has_low_row & jnp.logical_not(far_low), has_high_row & jnp.logical_not(far_high))
        + (hears_low, hears_high, has_low_col, has_high_col)
    )
    pl.semaphore_wait(barrier, sum(has.astype(jnp.int32) for has in expected))
    for has, step in ((hears_high, 1), (hears_low, -1)):

        @pl.when(has)
        def _(step=step):
            pl.semaphore_signal(
                told, inc=1, device_id={"row": lax.axis_index("row") + step}, device_id_type=MESH
            )

    def exchange(axis, has_low, has_high, up, down, from_low, from_high, sem):
        here = lax.axis_index(axis)
        to_high = pltpu.make_async_remote_copy(
            up, from_low, sem.at[0], sem.at[1], device_id={axis: here + 1}, device_id_type=MESH
        )
        to_low = pltpu.make_async_remote_copy(
            down, from_high, sem.at[2], sem.at[3], device_id={axis: here - 1}, device_id_type=MESH
        )
        def arrive():
            pl.when(has_low)(to_high.wait_recv)
            pl.when(has_high)(to_low.wait_recv)

        def sent():
            pl.when(has_high)(to_high.wait_send)
            pl.when(has_low)(to_low.wait_send)

        return to_high, to_low, arrive, sent

    v_high, v_low, v_arrive, v_sent = exchange(
        "col", has_low_col, has_high_col, vsend_up, vsend_down, vfrom_low, vfrom_high, v_sem
    )
    pl.when(has_low_col)(v_low.start)
    pl.when(has_high_col)(v_high.start)

    half = width // 2
    near = lax.broadcasted_iota(jnp.int32, (1, 128), 1)

    def across_middle(out, left, right):
        before = out[0][:, half // 2 - 128 :] + jnp.where(near == 127, 0.0625 * pltpu.roll(right, 127, 1), 0.0)
        after = out[1][:, :128] + jnp.where(
            near == 0, 0.0625 * pltpu.roll(left, 2, 1) + 0.25 * pltpu.roll(left, 1, 1), 0.0
        )
        return jnp.concatenate([out[0][:, : half // 2 - 128], before], 1), jnp.concatenate(
            [after, out[1][:, 128:]], 1
        )

    for copy in row_loads:
        copy.wait()
    spilled = []
    for b in range(bands):
        high, low = split(strip[b])
        z = dot(rt[...], jnp.concatenate([high, low, high], 0))
        for i in range(tiles):
            zown[b, i] = z[16:32, 128 * i : 128 * i + 128]
        spilled.append(z[0:16])
    spilled = jnp.concatenate(spilled, 0)
    count = spilled.shape[0]
    high, low = split(spilled)
    one = dot(
        jnp.concatenate([high[:, :half], low[:, :half], high[:, half:], low[:, half:]], 0), c1[...]
    )
    one = across_middle(
        (one[:count] + one[count : 2 * count], one[2 * count : 3 * count] + one[3 * count :]),
        spilled[:, half - 128 : half],
        spilled[:, half : half + 128],
    )
    two = dot(jnp.concatenate([high, low], 0), c12[...])
    two = two[:count] + two[count:]
    three = dot_split(two, c3[...])
    four = dot_split(three, c4[...])
    for b in range(bands):
        for side, target in enumerate((zsend_up, zsend_down)):
            g = slice(16 * b + 8 * side, 16 * b + 8 * side + 8)
            pad = jnp.zeros((8, width // 4 - 128), jnp.float32)
            group = lax.broadcasted_iota(jnp.int32, (8, width // 4), 0)
            packed = jnp.where(group < 6, jnp.concatenate([three[g], pad], 1), jnp.concatenate([four[g], pad], 1))
            packed = jnp.where(group < 4, two[g], packed)
            packed = jnp.where(group == 1, pltpu.roll(one[1][g], 1, 0), packed)
            target[b] = jnp.where(group == 0, one[0][g], packed)
    pl.when(far_high | far_low)(lambda: pl.semaphore_wait(told, 1))
    z_high, z_low, z_arrive, z_sent = exchange(
        "row", has_low_row, has_high_row, zsend_up, zsend_down, zfrom_low, zfrom_high, z_sem
    )
    pl.when(has_high_row)(z_high.start)
    pl.when(has_low_row)(z_low.start)
    e_high, e_low, e_arrive, e_sent = exchange(
        "row", has_low_row, has_high_row, esend, esend, efrom_low, efrom_high, e_sem
    )

    def forward():
        v_arrive()
        low = jnp.where(has_low_col, vfrom_low[...], 0.0)
        high = jnp.where(has_high_col, vfrom_high[...], 0.0)
        for b in range(bands):
            own = vown[b]
            first = pltpu.roll(own, 6, 0) + pltpu.roll(low, (8 - 2 * b) % 8, 0)
            last = pltpu.roll(own, 3, 0) + pltpu.roll(high, 7 - b, 0)
            both = jnp.where(row < 2, first, jnp.where(row == 7, last, 0.0))
            vown[b] = both
            esend[b] = both[:, height:]
        pl.when(has_high_row)(e_high.start)
        pl.when(has_low_row)(e_low.start)

    def reduce_band(b, carry):
        pl.when(late & (b == EARLY))(forward)
        for i in range(1, tiles - 1):
            tile_copy(b, i).wait()

        def reduce_tile(i, carry):
            for source, target in zip(fields[:LEVELS], ys):
                size = target.shape[2] - 2 * PAD
                tap = [source[b, i, pl.ds(PAD - 2 + t, size, stride=2)] for t in range(5)]
                target[b, i, PAD : PAD + size] = (
                    0.0625 * (tap[0] + tap[4]) + 0.25 * (tap[1] + tap[3]) + 0.375 * tap[2]
                )
            for k, y in enumerate(ys):
                y[b, i, PAD : PAD + 2] = y[b, i, PAD : PAD + 2] + zown[b, i, 2 * k : 2 * k + 2]
                end = slice(PAD + sizes[k] - 1, PAD + sizes[k])
                y[b, i, end] = y[b, i, end] + zown[b, i, 8 + 2 * k : 9 + 2 * k]
            return carry

        lax.fori_loop(0, tiles, reduce_tile, 0, unroll=UNROLL)
        return carry

    late = c >= cols_n // 2
    lax.fori_loop(0, bands, reduce_band, 0)
    pl.when(jnp.logical_not(late))(forward)

    rest = sum(sizes[1:])
    at = lax.broadcasted_iota(jnp.int32, (128, 128), 1)

    def reduce_columns(b, carry):
        base = 0
        for k in range(LEVELS):
            for i in range(tiles):
                high, low = split(ys[k][b, i, PAD : PAD + sizes[k]])
                if k == 0:
                    h, lanes = divmod(128 * i, half)
                    s1[2 * h * sizes[0] : (2 * h + 1) * sizes[0], lanes : lanes + 128] = high
                    s1[(2 * h + 1) * sizes[0] : (2 * h + 2) * sizes[0], lanes : lanes + 128] = low
                else:
                    s234[base : base + sizes[k], 128 * i : 128 * i + 128] = high
                    s234[rest + base : rest + base + sizes[k], 128 * i : 128 * i + 128] = low
            base += sizes[k] if k else 0
        one = dot(s1[...], c1[...])
        size = sizes[0]
        one = across_middle(
            (one[:size] + one[size : 2 * size], one[2 * size : 3 * size] + one[3 * size :]),
            y1[b, tiles // 2 - 1, PAD : PAD + size],
            y1[b, tiles // 2, PAD : PAD + size],
        )
        o1[b, :, : half // 2] = one[0]
        o1[b, :, half // 2 :] = one[1]
        two = dot(s234[...], c12[...])
        two = two[:rest] + two[rest:]
        three = dot_split(two[sizes[1] :], c3[...])
        four = dot_split(three[sizes[2] :], c4[...])
        o2[b] = two[: sizes[1]]
        o3[b] = three[: sizes[2]]
        o4[b] = four[:, : width >> 4]
        for part, levels in ((0, (0,)), (1, (1, 2, 3))):
            square = jnp.concatenate(
                [vown[b, :, 128 * part : 128 * part + 128], jnp.zeros((120, 128), jnp.float32)], 0
            ).T
            for k in levels:
                out = (o1, o2, o3, o4)[k]
                begin = starts[k] - 128 * part
                value = square[begin : begin + sizes[k]]
                tile = min(out.shape[2], 128)
                mark = at[: sizes[k]]
                low_cells = jnp.where(mark < 2, value, 0.0)[:, :tile]
                high_cells = jnp.where(mark == tile - 1, pltpu.roll(value, tile - 8, 1), 0.0)[:, :tile]
                out[b, :, 0:tile] = out[b, :, 0:tile] + low_cells
                out[b, :, out.shape[2] - tile :] = out[b, :, out.shape[2] - tile :] + high_cells
        return carry

    lax.fori_loop(0, bands, reduce_columns, 0)

    above = lax.broadcasted_iota(jnp.int32, (8, 128), 1) < 8
    z_arrive()
    for b in range(bands):
        low_rows[b] = jnp.where(has_low_row, zfrom_low[b], 0.0)
        high_rows[b] = jnp.where(has_high_row, zfrom_high[b], 0.0)
    e_arrive()
    for b in range(bands):
        corners[b] = jnp.where(
            above,
            jnp.where(has_low_row, efrom_low[b], 0.0),
            jnp.where(has_high_row, efrom_high[b], 0.0),
        )
    e_sent()
    z_sent()
    v_sent()


def store_kernel(a1, a2, a3, a4, low_rows, high_rows, corners, o1, o2, o3, o4, t1, t2, t3, t4, in_sem, edge_sem):
    bands = a1.shape[0]
    copies = []
    for k, (source, target) in enumerate(((a1, o1), (a2, o2), (a3, o3))):
        inner = slice(8, source.shape[1] - 8)
        copies.append(pltpu.make_async_copy(source.at[:, inner], target.at[:, inner], in_sem.at[k]))
        copies[-1].start()
    lane = lax.broadcasted_iota(jnp.int32, (16, 128), 1)
    for b in range(bands):
        cells = jnp.concatenate([corners[b], jnp.zeros((120, 128), jnp.float32)], 0).T[:16]
        first = jnp.where(lane < 2, cells, 0.0)
        last = jnp.where(lane == 127, pltpu.roll(cells, 120, 1), 0.0)
        last_half = jnp.where(lane == 63, pltpu.roll(cells, 56, 1), 0.0)
        for side, rows in enumerate((low_rows[b], high_rows[b])):
            for k, (source, target) in enumerate(zip((a1, a2, a3, a4), (t1, t2, t3, t4))):
                size, wide = source.shape[1:]
                count = 2 if side == 0 and k > 0 else 1
                at = slice(8 * side + 2 * k, 8 * side + 2 * k + count)
                if k == 0:
                    none = jnp.zeros((1, wide - 256), jnp.float32)
                    more = jnp.concatenate([rows[0:1], rows[1:2]], 1)
                    more = more + jnp.concatenate([first[at], none, last[at]], 1)
                else:
                    more = rows[2 * k : 2 * k + count, :wide]
                    if k == 1:
                        more = more + jnp.concatenate([first[at], last[at]], 1)
                    elif k == 2:
                        more = more + first[at] + last[at]
                    else:
                        more = more + (first[at] + last_half[at])[:, :wide]
                still = jnp.zeros((8 - count, wide), jnp.float32)
                if side == 0:
                    target[side, b] = source[b, 0:8] + jnp.concatenate([more, still], 0)
                else:
                    target[side, b] = source[b, size - 8 : size] + jnp.concatenate([still, more], 0)
    for k, (source, target) in enumerate(((t1, o1), (t2, o2), (t3, o3), (t4, o4))):
        size = target.shape[1]
        for side, begin in enumerate((0, size - 8)):
            copies.append(
                pltpu.make_async_copy(source.at[side], target.at[:, begin : begin + 8], edge_sem.at[side, k])
            )
            copies[-1].start()
    for copy in copies:
        copy.wait()


def solution(mesh):
    rows_n, cols_n = mesh.shape["row"], mesh.shape["col"]
    row_table, col_table = tables()
    all_rows = whole_rows(256)

    def local(relief):
        bands, height, width = relief.shape
        f32, bf16 = jnp.float32, jnp.bfloat16
        c1 = reduce_matrix(width // 2, False).T
        c12 = chain(width, False)[1].T
        c3 = reduce_matrix(width // 4, False).T
        c4 = np.zeros((width // 8, 128))
        c4[:, : width // 16] = reduce_matrix(width // 8, False).T
        consts = [jnp.asarray(a, bf16) for a in (row_table, col_table, all_rows, c1, c12, c3, c4)]
        shapes = [(bands, height >> k, width >> k) for k in range(1, LEVELS + 1)]

        vmem = lambda *shape, dtype=f32: pltpu.VMEM(shape, dtype)
        scratch = [vmem(bands, 2 * ROW_STRIP, width)]
        scratch += [vmem(bands, width // 128, (height >> k) + 2 * PAD, 128) for k in range(LEVELS + 1)]
        rest = sum(height >> k for k in range(2, LEVELS + 1))
        scratch += [
            vmem(2 * height, width // 2, dtype=bf16), vmem(2 * rest, width, dtype=bf16),
        ]
        scratch += [vmem(*a.shape, dtype=bf16) for a in (row_table[0], col_table[0], all_rows[0], c1, c12, c3, c4)]
        scratch += [vmem(bands, width // 128, 16, 128)]
        scratch += [vmem(bands, 8, width // 4)] * 4
        scratch += [vmem(bands, 8, 128)] * 3
        scratch += [vmem(bands, 8, height + 128)] + [vmem(8, height + 128)] * 4
        scratch += [
            pltpu.SemaphoreType.DMA(n) for n in ((2, bands), (bands, width // 128), (7,), (4,), (4,), (4,))
        ]
        scratch += [pltpu.SemaphoreType.REGULAR]
        extra = [(bands, 8, width // 4)] * 2 + [(bands, 8, 128)]
        held = pl.pallas_call(
            functools.partial(pyramid_kernel, rows_n, cols_n),
            out_shape=[jax.ShapeDtypeStruct(s, f32) for s in shapes + extra],
            in_specs=[pl.BlockSpec(memory_space=pltpu.HBM)] * 8,
            out_specs=[pl.BlockSpec(memory_space=pltpu.VMEM)] * (LEVELS + 3),
            scratch_shapes=scratch,
            compiler_params=pltpu.CompilerParams(
                collective_id=0, has_side_effects=True, vmem_limit_bytes=40 << 20
            ),
            name="pyramid",
        )(*[pltpu.with_memory_space_constraint(a, pltpu.HBM) for a in (relief, *consts)])
        return pl.pallas_call(
            store_kernel,
            out_shape=[jax.ShapeDtypeStruct(s, f32) for s in shapes],
            in_specs=[pl.BlockSpec(memory_space=pltpu.VMEM)] * (LEVELS + 3),
            out_specs=[pl.BlockSpec(memory_space=pltpu.HBM)] * LEVELS,
            scratch_shapes=[vmem(2, bands, 8, across) for _, _, across in shapes]
            + [pltpu.SemaphoreType.DMA((LEVELS - 1,)), pltpu.SemaphoreType.DMA((2, LEVELS))],
            compiler_params=pltpu.CompilerParams(vmem_limit_bytes=16 << 20),
            name="store",
        )(*held)

    spec = P(None, "row", "col")
    return jax.shard_map(local, mesh=mesh, in_specs=(spec,), out_specs=(spec,) * LEVELS, check_vma=False)
```

```python
import functools

import jax
import jax.numpy as jnp
import numpy as np
from jax import lax
from jax.experimental import pallas as pl
from jax.experimental.pallas import tpu as pltpu
from jax.sharding import PartitionSpec as P

MESH = pl.DeviceIdType.MESH
BINOMIAL = np.array([1, 4, 6, 4, 1]) / 16
LEVELS = 4
PAD = 8
ROW_STRIP = 32
COL_STRIP = 64
UNROLL = 2
EARLY = 1


def reduce_matrix(n, reflect):
    d = np.zeros((n // 2, n))
    for i in range(n // 2):
        for t in range(5):
            c = 2 * i - 2 + t
            if c < 0 or c >= n:
                if not reflect:
                    continue
                c = -c if c < 0 else 2 * (n - 1) - c
            d[i, c] += BINOMIAL[t]
    return d


def chain(n, reflect):
    out, m = [], np.eye(n)
    for _ in range(LEVELS):
        m = reduce_matrix(m.shape[0], reflect) @ m
        out.append(m)
    return out


def edge_parts(n):
    whole, alone = chain(3 * n, True), chain(n, False)
    places = []
    for p in range(3):
        parts = []
        for k in range(LEVELS):
            m = n >> (k + 1)
            mine = whole[k][:, p * n : (p + 1) * n]
            own = mine[p * m : (p + 1) * m] - alone[k]
            assert not own[2:-1].any()
            up = mine[(p + 1) * m : (p + 1) * m + 2] if p < 2 else np.zeros((2, n))
            down = mine[p * m - 1 : p * m] if p > 0 else np.zeros((1, n))
            parts.append((up, down, own[:2], own[-1:]))
        places.append(parts)
    return places


def ends(rows, strip):
    return np.concatenate([rows[:, :strip], rows[:, -strip:]], 1)


def parts_of(table):
    high = np.asarray(jnp.asarray(table, jnp.bfloat16), np.float32)
    return high, table - high


def tables():
    places = edge_parts(256)
    row_table = np.zeros((3, 32, 2 * ROW_STRIP), np.float32)
    col_table = np.zeros((3, 8 * LEVELS, 2 * COL_STRIP), np.float32)
    for p, parts in enumerate(places):
        for k, (up, down, first, last) in enumerate(parts):
            row_table[p, 2 * k : 2 * k + 2] = ends(up, ROW_STRIP)
            row_table[p, 8 + 2 * k] = ends(down, ROW_STRIP)[0]
            row_table[p, 16 + 2 * k : 18 + 2 * k] = ends(first, ROW_STRIP)
            row_table[p, 24 + 2 * k] = ends(last, ROW_STRIP)[0]
            col_table[p, 8 * k : 8 * k + 6] = ends(np.concatenate([up, first, last, down]), COL_STRIP)
    high, low = parts_of(row_table)
    row_table = np.concatenate([high, high, low], 2)
    high, low = parts_of(col_table)
    none = np.zeros_like(low)
    col_table = np.concatenate(
        [np.concatenate([high, high], 2), np.concatenate([low, none], 2)], 1
    )
    return row_table, col_table


ABOVE = ((0, 1), (2, 3), (4, 5), (6, 7))
BELOW = (8, 10, 12, 14)


def whole_rows(n):
    whole = chain(3 * n, True)
    table = np.zeros((3, n, n + 128), np.float32)
    for p in range(3):
        for k in range(LEVELS):
            m, begin = n >> (k + 1), n - (n >> k)
            mine = whole[k][:, p * n : (p + 1) * n]
            table[p, :, begin : begin + m] = mine[p * m : (p + 1) * m].T
            if p < 2:
                for lane, cells in zip(ABOVE[k], mine[(p + 1) * m :]):
                    table[p, :, n + lane] = cells
            if p > 0:
                table[p, :, n + BELOW[k]] = mine[p * m - 1]
    return np.stack(parts_of(table), 1)


def split(a):
    high = a.astype(jnp.bfloat16)
    return high, (a - high.astype(jnp.float32)).astype(jnp.bfloat16)


dot = functools.partial(jnp.dot, preferred_element_type=jnp.float32)


def dot_split(a, weights):
    high, low = split(a)
    return dot(high, weights) + dot(low, weights)


def place(index, count):
    return jnp.where(index == 0, 0, jnp.where(index == count - 1, 2, 1))


def pyramid_kernel(
    rows_n, cols_n, x_hbm, rt_hbm, ct_hbm, wr_hbm, cc_hbm,
    o1, o2, o3, o4, low_rows, high_rows, corners,
    strip, x, y1, y2, y3, y4, s1, s234, rt, ct, wr, cc, zown,
    zsend_up, zsend_down, zfrom_low, zfrom_high,
    esend, efrom_low, efrom_high,
    vown, vsend_up, vsend_down, vfrom_low, vfrom_high,
    s_sem, x_sem, t_sem, e_sem, z_sem, v_sem, told,
):
    bands, height, width = x_hbm.shape
    tiles = width // 128
    r, c = lax.axis_index("row"), lax.axis_index("col")
    has_low_row, has_high_row = r > 0, r < rows_n - 1
    has_low_col, has_high_col = c > 0, c < cols_n - 1
    ys = (y1, y2, y3, y4)
    fields = (x,) + ys
    sizes = [height >> (k + 1) for k in range(LEVELS)]
    starts = [height - (height >> k) for k in range(LEVELS)]

    place_in_line = r % 8
    far_high = (place_in_line == 7) & has_high_row
    far_low = (place_in_line == 0) & has_low_row
    hears_high = (place_in_line == 6) & (r + 2 < rows_n)
    hears_low = (place_in_line == 1) & (r > 1)
    barrier = pltpu.get_barrier_semaphore()
    for axis, has, step in (
        ("row", has_low_row & jnp.logical_not(far_low), -1), ("row", has_high_row & jnp.logical_not(far_high), 1),
        ("row", far_low, -2), ("row", far_high, 2),
        ("col", has_low_col, -1), ("col", has_high_col, 1),
    ):

        @pl.when(has)
        def _(axis=axis, step=step):
            pl.semaphore_signal(
                barrier, inc=1, device_id={axis: lax.axis_index(axis) + step}, device_id_type=MESH
            )

    def load(source, target, sem):
        copy = pltpu.make_async_copy(source, target, sem)
        copy.start()
        return copy

    def load_tile(i, sem):
        return load(x_hbm.at[:, :, 128 * i : 128 * i + 128], x.at[:, i, PAD : PAD + height], sem)

    col_loads = [
        load(ct_hbm.at[place(c, cols_n)], ct, t_sem.at[0]),
        load_tile(0, x_sem.at[0]),
        load_tile(tiles - 1, x_sem.at[1]),
    ]
    wr_load = load(wr_hbm.at[place(r, rows_n)], wr, t_sem.at[1])

    for field in fields[:LEVELS]:
        size = field.shape[2] - 2 * PAD
        zeros = jnp.zeros((bands, tiles, PAD, 128), jnp.float32)
        field[:, :, 0:PAD] = zeros
        field[:, :, PAD + size :] = zeros

    lower_half = lax.broadcasted_iota(jnp.int32, (1, 128), 1) < 64
    for copy in col_loads:
        copy.wait()
    row_loads = [load(rt_hbm.at[place(r, rows_n)], rt, t_sem.at[2])]
    for e, begin in enumerate((0, height - ROW_STRIP)):
        row_loads.append(
            load(
                x_hbm.at[:, begin : begin + ROW_STRIP],
                strip.at[:, e * ROW_STRIP : (e + 1) * ROW_STRIP],
                s_sem.at[e],
            )
        )
    row_loads.append(load(cc_hbm, cc, t_sem.at[3]))
    for i in range(1, tiles - 1):
        load_tile(i, x_sem.at[2])
    c12, c1 = cc.at[0:width], cc.at[width : width + width // 2]
    tail = width + width // 2
    c3, c4 = cc.at[tail : tail + width // 4, 0:128], cc.at[tail : tail + width // 8, 128:256]
    parts = []
    for b in range(bands):
        parts.append(
            jnp.concatenate(
                split(
                    jnp.where(lower_half, x[b, 0, PAD : PAD + height], x[b, tiles - 1, PAD : PAD + height])
                ),
                1,
            )
        )
    v = lax.dot_general(
        ct[...],
        jnp.concatenate(parts, 0),
        (((1,), (1,)), ((), ())),
        preferred_element_type=jnp.float32,
    )
    v = v[: 8 * LEVELS] + v[8 * LEVELS :]
    raw = [v[:, b * height : (b + 1) * height] for b in range(bands)]
    raw = jnp.concatenate(raw, 0)
    wr_load.wait()
    high, low = split(raw)
    v = dot(jnp.concatenate([high, low], 0), wr[0])
    v = v[: raw.shape[0]] + v[raw.shape[0] :] + dot(high, wr[1])
    lane = lax.broadcasted_iota(jnp.int32, (8, height + 128), 1)
    row = lax.broadcasted_iota(jnp.int32, (8, height + 128), 0)
    beyond = lane - height
    level_of = jnp.where(
        lane < height,
        sum((lane >= start).astype(jnp.int32) for start in starts[1:]),
        (beyond & 7) >> 1,
    )
    up, down = jnp.zeros(lane.shape, jnp.float32), jnp.zeros(lane.shape, jnp.float32)
    for b in range(bands):
        begin = 8 * LEVELS * b
        picked = v[begin : begin + 8]
        for k in range(1, LEVELS):
            picked = jnp.where(level_of == k, v[begin + 8 * k : begin + 8 * k + 8], picked)
        vown[b] = picked
        up = jnp.where((row >= 2 * b) & (row < 2 * b + 2), pltpu.roll(picked, 2 * b, 0), up)
        down = jnp.where(row == b, pltpu.roll(picked, b + 3, 0), down)
    vsend_up[...] = up
    vsend_down[...] = down

    expected = (
        (has_low_row & jnp.logical_not(far_low), has_high_row & jnp.logical_not(far_high))
        + (hears_low, hears_high, has_low_col, has_high_col)
    )
    pl.semaphore_wait(barrier, sum(has.astype(jnp.int32) for has in expected))
    for has, step in ((hears_high, 1), (hears_low, -1)):

        @pl.when(has)
        def _(step=step):
            pl.semaphore_signal(
                told, inc=1, device_id={"row": lax.axis_index("row") + step}, device_id_type=MESH
            )

    def exchange(axis, has_low, has_high, up, down, from_low, from_high, sem):
        here = lax.axis_index(axis)
        to_high = pltpu.make_async_remote_copy(
            up, from_low, sem.at[0], sem.at[1], device_id={axis: here + 1}, device_id_type=MESH
        )
        to_low = pltpu.make_async_remote_copy(
            down, from_high, sem.at[2], sem.at[3], device_id={axis: here - 1}, device_id_type=MESH
        )
        def arrive():
            pl.when(has_low)(to_high.wait_recv)
            pl.when(has_high)(to_low.wait_recv)

        def sent():
            pl.when(has_high)(to_high.wait_send)
            pl.when(has_low)(to_low.wait_send)

        return to_high, to_low, arrive, sent

    v_high, v_low, v_arrive, v_sent = exchange(
        "col", has_low_col, has_high_col, vsend_up, vsend_down, vfrom_low, vfrom_high, v_sem
    )
    pl.when(has_low_col)(v_low.start)
    pl.when(has_high_col)(v_high.start)

    half = width // 2
    near = lax.broadcasted_iota(jnp.int32, (1, 128), 1)

    def across_middle(out, left, right):
        before = out[0][:, half // 2 - 128 :] + jnp.where(near == 127, 0.0625 * pltpu.roll(right, 127, 1), 0.0)
        after = out[1][:, :128] + jnp.where(
            near == 0, 0.0625 * pltpu.roll(left, 2, 1) + 0.25 * pltpu.roll(left, 1, 1), 0.0
        )
        return jnp.concatenate([out[0][:, : half // 2 - 128], before], 1), jnp.concatenate(
            [after, out[1][:, 128:]], 1
        )

    for copy in row_loads:
        copy.wait()
    spilled = []
    for b in range(bands):
        high, low = split(strip[b])
        z = dot(rt[...], jnp.concatenate([high, low, high], 0))
        for i in range(tiles):
            zown[b, i] = z[16:32, 128 * i : 128 * i + 128]
        spilled.append(z[0:16])
    spilled = jnp.concatenate(spilled, 0)
    count = spilled.shape[0]
    high, low = split(spilled)
    one = dot(
        jnp.concatenate([high[:, :half], low[:, :half], high[:, half:], low[:, half:]], 0), c1[...]
    )
    one = across_middle(
        (one[:count] + one[count : 2 * count], one[2 * count : 3 * count] + one[3 * count :]),
        spilled[:, half - 128 : half],
        spilled[:, half : half + 128],
    )
    two = dot(jnp.concatenate([high, low], 0), c12[...])
    two = two[:count] + two[count:]
    three = dot_split(two, c3[...])
    four = dot_split(three, c4[...])
    for b in range(bands):
        for side, target in enumerate((zsend_up, zsend_down)):
            g = slice(16 * b + 8 * side, 16 * b + 8 * side + 8)
            pad = jnp.zeros((8, width // 4 - 128), jnp.float32)
            group = lax.broadcasted_iota(jnp.int32, (8, width // 4), 0)
            packed = jnp.where(group < 6, jnp.concatenate([three[g], pad], 1), jnp.concatenate([four[g], pad], 1))
            packed = jnp.where(group < 4, two[g], packed)
            packed = jnp.where(group == 1, pltpu.roll(one[1][g], 1, 0), packed)
            target[b] = jnp.where(group == 0, one[0][g], packed)
    pl.when(far_high | far_low)(lambda: pl.semaphore_wait(told, 1))
    z_high, z_low, z_arrive, z_sent = exchange(
        "row", has_low_row, has_high_row, zsend_up, zsend_down, zfrom_low, zfrom_high, z_sem
    )
    pl.when(has_high_row)(z_high.start)
    pl.when(has_low_row)(z_low.start)
    e_high, e_low, e_arrive, e_sent = exchange(
        "row", has_low_row, has_high_row, esend, esend, efrom_low, efrom_high, e_sem
    )

    def forward():
        v_arrive()
        low = jnp.where(has_low_col, vfrom_low[...], 0.0)
        high = jnp.where(has_high_col, vfrom_high[...], 0.0)
        for b in range(bands):
            own = vown[b]
            first = pltpu.roll(own, 6, 0) + pltpu.roll(low, (8 - 2 * b) % 8, 0)
            last = pltpu.roll(own, 3, 0) + pltpu.roll(high, 7 - b, 0)
            both = jnp.where(row < 2, first, jnp.where(row == 7, last, 0.0))
            vown[b] = both
            esend[b] = both[:, height:]
        pl.when(has_high_row)(e_high.start)
        pl.when(has_low_row)(e_low.start)

    def reduce_band(b, carry):
        pl.when(late & (b == EARLY))(forward)
        def reduce_tile(i, carry):
            for source, target in zip(fields[:LEVELS], ys):
                size = target.shape[2] - 2 * PAD
                tap = [source[b, i, pl.ds(PAD - 2 + t, size, stride=2)] for t in range(5)]
                target[b, i, PAD : PAD + size] = (
                    0.0625 * (tap[0] + tap[4]) + 0.25 * (tap[1] + tap[3]) + 0.375 * tap[2]
                )
            for k, y in enumerate(ys):
                y[b, i, PAD : PAD + 2] = y[b, i, PAD : PAD + 2] + zown[b, i, 2 * k : 2 * k + 2]
                end = slice(PAD + sizes[k] - 1, PAD + sizes[k])
                y[b, i, end] = y[b, i, end] + zown[b, i, 8 + 2 * k : 9 + 2 * k]
            return carry

        lax.fori_loop(0, tiles, reduce_tile, 0, unroll=UNROLL)
        return carry

    late = c >= cols_n // 2
    inner = x.at[:, 1 : tiles - 1, PAD : PAD + height]
    pltpu.make_async_copy(inner, inner, x_sem.at[2]).wait()
    lax.fori_loop(0, bands, reduce_band, 0)
    pl.when(jnp.logical_not(late))(forward)

    rest = sum(sizes[1:])
    at = lax.broadcasted_iota(jnp.int32, (128, 128), 1)

    def reduce_columns(b, carry):
        base = 0
        for k in range(LEVELS):
            for i in range(tiles):
                high, low = split(ys[k][b, i, PAD : PAD + sizes[k]])
                if k == 0:
                    h, lanes = divmod(128 * i, half)
                    s1[2 * h * sizes[0] : (2 * h + 1) * sizes[0], lanes : lanes + 128] = high
                    s1[(2 * h + 1) * sizes[0] : (2 * h + 2) * sizes[0], lanes : lanes + 128] = low
                else:
                    s234[base : base + sizes[k], 128 * i : 128 * i + 128] = high
                    s234[rest + base : rest + base + sizes[k], 128 * i : 128 * i + 128] = low
            base += sizes[k] if k else 0
        one = dot(s1[...], c1[...])
        size = sizes[0]
        one = across_middle(
            (one[:size] + one[size : 2 * size], one[2 * size : 3 * size] + one[3 * size :]),
            y1[b, tiles // 2 - 1, PAD : PAD + size],
            y1[b, tiles // 2, PAD : PAD + size],
        )
        o1[b, :, : half // 2] = one[0]
        o1[b, :, half // 2 :] = one[1]
        two = dot(s234[...], c12[...])
        two = two[:rest] + two[rest:]
        three = dot_split(two[sizes[1] :], c3[...])
        four = dot_split(three[sizes[2] :], c4[...])
        o2[b] = two[: sizes[1]]
        o3[b] = three[: sizes[2]]
        o4[b] = four[:, : width >> 4]
        for part, levels in ((0, (0,)), (1, (1, 2, 3))):
            square = jnp.concatenate(
                [vown[b, :, 128 * part : 128 * part + 128], jnp.zeros((120, 128), jnp.float32)], 0
            ).T
            for k in levels:
                out = (o1, o2, o3, o4)[k]
                begin = starts[k] - 128 * part
                value = square[begin : begin + sizes[k]]
                tile = min(out.shape[2], 128)
                mark = at[: sizes[k]]
                low_cells = jnp.where(mark < 2, value, 0.0)[:, :tile]
                high_cells = jnp.where(mark == tile - 1, pltpu.roll(value, tile - 8, 1), 0.0)[:, :tile]
                out[b, :, 0:tile] = out[b, :, 0:tile] + low_cells
                out[b, :, out.shape[2] - tile :] = out[b, :, out.shape[2] - tile :] + high_cells
        return carry

    lax.fori_loop(0, bands, reduce_columns, 0)

    above = lax.broadcasted_iota(jnp.int32, (8, 128), 1) < 8
    z_arrive()
    for b in range(bands):
        low_rows[b] = jnp.where(has_low_row, zfrom_low[b], 0.0)
        high_rows[b] = jnp.where(has_high_row, zfrom_high[b], 0.0)
    e_arrive()
    for b in range(bands):
        corners[b] = jnp.where(
            above,
            jnp.where(has_low_row, efrom_low[b], 0.0),
            jnp.where(has_high_row, efrom_high[b], 0.0),
        )
    e_sent()
    z_sent()
    v_sent()


def store_kernel(a1, a2, a3, a4, low_rows, high_rows, corners, o1, o2, o3, o4, t1, t2, t3, t4, in_sem, edge_sem):
    bands = a1.shape[0]
    copies = []
    for k, (source, target) in enumerate(((a1, o1), (a2, o2), (a3, o3))):
        inner = slice(8, source.shape[1] - 8)
        copies.append(pltpu.make_async_copy(source.at[:, inner], target.at[:, inner], in_sem.at[k]))
        copies[-1].start()
    lane = lax.broadcasted_iota(jnp.int32, (16, 128), 1)
    for b in range(bands):
        cells = jnp.concatenate([corners[b], jnp.zeros((120, 128), jnp.float32)], 0).T[:16]
        first = jnp.where(lane < 2, cells, 0.0)
        last = jnp.where(lane == 127, pltpu.roll(cells, 120, 1), 0.0)
        last_half = jnp.where(lane == 63, pltpu.roll(cells, 56, 1), 0.0)
        for side, rows in enumerate((low_rows[b], high_rows[b])):
            for k, (source, target) in enumerate(zip((a1, a2, a3, a4), (t1, t2, t3, t4))):
                size, wide = source.shape[1:]
                count = 2 if side == 0 and k > 0 else 1
                at = slice(8 * side + 2 * k, 8 * side + 2 * k + count)
                if k == 0:
                    none = jnp.zeros((1, wide - 256), jnp.float32)
                    more = jnp.concatenate([rows[0:1], rows[1:2]], 1)
                    more = more + jnp.concatenate([first[at], none, last[at]], 1)
                else:
                    more = rows[2 * k : 2 * k + count, :wide]
                    if k == 1:
                        more = more + jnp.concatenate([first[at], last[at]], 1)
                    elif k == 2:
                        more = more + first[at] + last[at]
                    else:
                        more = more + (first[at] + last_half[at])[:, :wide]
                still = jnp.zeros((8 - count, wide), jnp.float32)
                if side == 0:
                    target[side, b] = source[b, 0:8] + jnp.concatenate([more, still], 0)
                else:
                    target[side, b] = source[b, size - 8 : size] + jnp.concatenate([still, more], 0)
    for k, (source, target) in enumerate(((t1, o1), (t2, o2), (t3, o3), (t4, o4))):
        size = target.shape[1]
        for side, begin in enumerate((0, size - 8)):
            pltpu.make_async_copy(source.at[side], target.at[:, begin : begin + 8], edge_sem.at[k]).start()
        copies.append(pltpu.make_async_copy(source, source, edge_sem.at[k]))
    for copy in copies:
        copy.wait()


def solution(mesh):
    rows_n, cols_n = mesh.shape["row"], mesh.shape["col"]
    row_table, col_table = tables()
    all_rows = whole_rows(256)

    def local(relief):
        bands, height, width = relief.shape
        f32, bf16 = jnp.float32, jnp.bfloat16
        c1 = reduce_matrix(width // 2, False).T
        c12 = chain(width, False)[1].T
        c3 = reduce_matrix(width // 4, False).T
        c4 = np.zeros((width // 4, 128))
        c4[: width // 8, : width // 16] = reduce_matrix(width // 8, False).T
        cc = np.concatenate([c12, c1, np.concatenate([c3, c4], 1)], 0)
        consts = [jnp.asarray(a, bf16) for a in (row_table, col_table, all_rows, cc)]
        shapes = [(bands, height >> k, width >> k) for k in range(1, LEVELS + 1)]

        vmem = lambda *shape, dtype=f32: pltpu.VMEM(shape, dtype)
        scratch = [vmem(bands, 2 * ROW_STRIP, width)]
        scratch += [vmem(bands, width // 128, (height >> k) + 2 * PAD, 128) for k in range(LEVELS + 1)]
        rest = sum(height >> k for k in range(2, LEVELS + 1))
        scratch += [
            vmem(2 * height, width // 2, dtype=bf16), vmem(2 * rest, width, dtype=bf16),
        ]
        scratch += [vmem(*a.shape, dtype=bf16) for a in (row_table[0], col_table[0], all_rows[0], cc)]
        scratch += [vmem(bands, width // 128, 16, 128)]
        scratch += [vmem(bands, 8, width // 4)] * 4
        scratch += [vmem(bands, 8, 128)] * 3
        scratch += [vmem(bands, 8, height + 128)] + [vmem(8, height + 128)] * 4
        scratch += [
            pltpu.SemaphoreType.DMA(n) for n in ((2,), (3,), (4,), (4,), (4,), (4,))
        ]
        scratch += [pltpu.SemaphoreType.REGULAR]
        extra = [(bands, 8, width // 4)] * 2 + [(bands, 8, 128)]
        held = pl.pallas_call(
            functools.partial(pyramid_kernel, rows_n, cols_n),
            out_shape=[jax.ShapeDtypeStruct(s, f32) for s in shapes + extra],
            in_specs=[pl.BlockSpec(memory_space=pltpu.HBM)] * 5,
            out_specs=[pl.BlockSpec(memory_space=pltpu.VMEM)] * (LEVELS + 3),
            scratch_shapes=scratch,
            compiler_params=pltpu.CompilerParams(
                collective_id=0, has_side_effects=True, vmem_limit_bytes=40 << 20
            ),
            name="pyramid",
        )(*[pltpu.with_memory_space_constraint(a, pltpu.HBM) for a in (relief, *consts)])
        return pl.pallas_call(
            store_kernel,
            out_shape=[jax.ShapeDtypeStruct(s, f32) for s in shapes],
            in_specs=[pl.BlockSpec(memory_space=pltpu.VMEM)] * (LEVELS + 3),
            out_specs=[pl.BlockSpec(memory_space=pltpu.HBM)] * LEVELS,
            scratch_shapes=[vmem(2, bands, 8, across) for _, _, across in shapes]
            + [pltpu.SemaphoreType.DMA((LEVELS - 1,)), pltpu.SemaphoreType.DMA((LEVELS,))],
            compiler_params=pltpu.CompilerParams(vmem_limit_bytes=16 << 20),
            name="store",
        )(*held)

    spec = P(None, "row", "col")
    return jax.shard_map(local, mesh=mesh, in_specs=(spec,), out_specs=(spec,) * LEVELS, check_vma=False)
```

```python
import functools

import jax
import jax.numpy as jnp
import numpy as np
from jax import lax
from jax.experimental import pallas as pl
from jax.experimental.pallas import tpu as pltpu
from jax.sharding import PartitionSpec as P

MESH = pl.DeviceIdType.MESH
BINOMIAL = np.array([1, 4, 6, 4, 1]) / 16
LEVELS = 4
PAD = 8
ROW_STRIP = 32
COL_STRIP = 64
UNROLL = 4
DIRECT = 4
FORWARD = 1
EARLY = 1


def reduce_matrix(n, reflect):
    d = np.zeros((n // 2, n))
    for i in range(n // 2):
        for t in range(5):
            c = 2 * i - 2 + t
            if c < 0 or c >= n:
                if not reflect:
                    continue
                c = -c if c < 0 else 2 * (n - 1) - c
            d[i, c] += BINOMIAL[t]
    return d


def chain(n, reflect):
    out, m = [], np.eye(n)
    for _ in range(LEVELS):
        m = reduce_matrix(m.shape[0], reflect) @ m
        out.append(m)
    return out


def edge_parts(n):
    whole, alone = chain(3 * n, True), chain(n, False)
    places = []
    for p in range(3):
        parts = []
        for k in range(LEVELS):
            m = n >> (k + 1)
            mine = whole[k][:, p * n : (p + 1) * n]
            own = mine[p * m : (p + 1) * m] - alone[k]
            assert not own[2:-1].any()
            up = mine[(p + 1) * m : (p + 1) * m + 2] if p < 2 else np.zeros((2, n))
            down = mine[p * m - 1 : p * m] if p > 0 else np.zeros((1, n))
            parts.append((up, down, own[:2], own[-1:]))
        places.append(parts)
    return places


def ends(rows, strip):
    return np.concatenate([rows[:, :strip], rows[:, -strip:]], 1)


def parts_of(table):
    high = np.asarray(jnp.asarray(table, jnp.bfloat16), np.float32)
    return high, table - high


def tables():
    places = edge_parts(256)
    row_table = np.zeros((3, 32, 2 * ROW_STRIP), np.float32)
    col_table = np.zeros((3, 8 * LEVELS, 2 * COL_STRIP), np.float32)
    for p, parts in enumerate(places):
        for k, (up, down, first, last) in enumerate(parts):
            row_table[p, 2 * k : 2 * k + 2] = ends(up, ROW_STRIP)
            row_table[p, 8 + 2 * k] = ends(down, ROW_STRIP)[0]
            row_table[p, 16 + 2 * k : 18 + 2 * k] = ends(first, ROW_STRIP)
            row_table[p, 24 + 2 * k] = ends(last, ROW_STRIP)[0]
            col_table[p, 8 * k : 8 * k + 6] = ends(np.concatenate([up, first, last, down]), COL_STRIP)
    high, low = parts_of(row_table)
    row_table = np.concatenate([high, high, low], 2)
    high, low = parts_of(col_table)
    none = np.zeros_like(low)
    col_table = np.concatenate(
        [np.concatenate([high, high], 2), np.concatenate([low, none], 2)], 1
    )
    return row_table, col_table


ABOVE = ((0, 1), (2, 3), (4, 5), (6, 7))
BELOW = (8, 10, 12, 14)


def whole_rows(n):
    whole = chain(3 * n, True)
    table = np.zeros((3, n, n + 128), np.float32)
    for p in range(3):
        for k in range(LEVELS):
            m, begin = n >> (k + 1), n - (n >> k)
            mine = whole[k][:, p * n : (p + 1) * n]
            table[p, :, begin : begin + m] = mine[p * m : (p + 1) * m].T
            if p < 2:
                for lane, cells in zip(ABOVE[k], mine[(p + 1) * m :]):
                    table[p, :, n + lane] = cells
            if p > 0:
                table[p, :, n + BELOW[k]] = mine[p * m - 1]
    return np.stack(parts_of(table), 1)


def split(a):
    high = a.astype(jnp.bfloat16)
    return high, (a - high.astype(jnp.float32)).astype(jnp.bfloat16)


dot = functools.partial(jnp.dot, preferred_element_type=jnp.float32)


def dot_split(a, weights):
    high, low = split(a)
    return dot(high, weights) + dot(low, weights)


def place(index, count):
    return jnp.where(index == 0, 0, jnp.where(index == count - 1, 2, 1))


def pyramid_kernel(
    rows_n, cols_n, x_hbm, rt_hbm, ct_hbm, wr_hbm, cc_hbm,
    o1, o2, o3, o4, low_rows, high_rows, corners,
    strip, x, y1, y2, y3, y4, s1, s234, rt, ct, wr, cc, zown,
    zsend_up, zsend_down, zfrom_low, zfrom_high,
    esend, efrom_low, efrom_high,
    vown, vsend_up, vsend_down, vfrom_low, vfrom_high, dfrom_low, dfrom_high,
    s_sem, x_sem, t_sem, e_sem, z_sem, v_sem, d_sem, told,
):
    bands, height, width = x_hbm.shape
    tiles = width // 128
    r, c = lax.axis_index("row"), lax.axis_index("col")
    has_low_row, has_high_row = r > 0, r < rows_n - 1
    has_low_col, has_high_col = c > 0, c < cols_n - 1
    ys = (y1, y2, y3, y4)
    fields = (x,) + ys
    sizes = [height >> (k + 1) for k in range(LEVELS)]
    starts = [height - (height >> k) for k in range(LEVELS)]

    place_in_line = r % 8
    far_high = (place_in_line == 7) & has_high_row
    far_low = (place_in_line == 0) & has_low_row
    hears_high = (place_in_line == 6) & (r + 2 < rows_n)
    hears_low = (place_in_line == 1) & (r > 1)
    middle = cols_n // 2
    direct = (c >= middle - DIRECT) & (c < middle) & has_high_col
    sends_diagonal = (c > middle - DIRECT) & (c <= middle) & has_low_col
    barrier = pltpu.get_barrier_semaphore()
    for axis, has, step in (
        ("row", has_low_row & jnp.logical_not(far_low), -1), ("row", has_high_row & jnp.logical_not(far_high), 1),
        ("row", far_low, -2), ("row", far_high, 2),
        ("col", has_low_col, -1), ("col", has_high_col, 1),
    ):

        @pl.when(has)
        def _(axis=axis, step=step):
            pl.semaphore_signal(
                barrier, inc=1, device_id={axis: lax.axis_index(axis) + step}, device_id_type=MESH
            )

    for has, step in ((has_low_row, -1), (has_high_row, 1)):

        @pl.when(has & direct)
        def _(step=step):
            pl.semaphore_signal(barrier, inc=1, device_id={"row": r + step, "col": c + 1}, device_id_type=MESH)

    def load(source, target, sem):
        copy = pltpu.make_async_copy(source, target, sem)
        copy.start()
        return copy

    def load_tile(i, sem):
        return load(x_hbm.at[:, :, 128 * i : 128 * i + 128], x.at[:, i, PAD : PAD + height], sem)

    col_loads = [
        load(ct_hbm.at[place(c, cols_n)], ct, t_sem.at[0]),
        load_tile(0, x_sem.at[0]),
        load_tile(tiles - 1, x_sem.at[1]),
    ]
    wr_load = load(wr_hbm.at[place(r, rows_n)], wr, t_sem.at[1])

    for field in fields[:LEVELS]:
        size = field.shape[2] - 2 * PAD
        zeros = jnp.zeros((bands, tiles, PAD, 128), jnp.float32)
        field[:, :, 0:PAD] = zeros
        field[:, :, PAD + size :] = zeros

    lower_half = lax.broadcasted_iota(jnp.int32, (1, 128), 1) < 64
    for copy in col_loads:
        copy.wait()
    row_loads = [load(rt_hbm.at[place(r, rows_n)], rt, t_sem.at[2])]
    for e, begin in enumerate((0, height - ROW_STRIP)):
        row_loads.append(
            load(
                x_hbm.at[:, begin : begin + ROW_STRIP],
                strip.at[:, e * ROW_STRIP : (e + 1) * ROW_STRIP],
                s_sem.at[e],
            )
        )
    row_loads.append(load(cc_hbm, cc, t_sem.at[3]))
    for i in range(1, tiles - 1):
        load_tile(i, x_sem.at[2])
    c12, c1 = cc.at[0:width], cc.at[width : width + width // 2]
    tail = width + width // 2
    c3, c4 = cc.at[tail : tail + width // 4, 0:128], cc.at[tail : tail + width // 8, 128:256]
    parts = []
    for b in range(bands):
        parts.append(
            jnp.concatenate(
                split(
                    jnp.where(lower_half, x[b, 0, PAD : PAD + height], x[b, tiles - 1, PAD : PAD + height])
                ),
                1,
            )
        )
    v = lax.dot_general(
        ct[...],
        jnp.concatenate(parts, 0),
        (((1,), (1,)), ((), ())),
        preferred_element_type=jnp.float32,
    )
    v = v[: 8 * LEVELS] + v[8 * LEVELS :]
    raw = [v[:, b * height : (b + 1) * height] for b in range(bands)]
    raw = jnp.concatenate(raw, 0)
    wr_load.wait()
    high, low = split(raw)
    v = dot(jnp.concatenate([high, low], 0), wr[0])
    v = v[: raw.shape[0]] + v[raw.shape[0] :] + dot(high, wr[1])
    lane = lax.broadcasted_iota(jnp.int32, (8, height + 128), 1)
    row = lax.broadcasted_iota(jnp.int32, (8, height + 128), 0)
    beyond = lane - height
    level_of = jnp.where(
        lane < height,
        sum((lane >= start).astype(jnp.int32) for start in starts[1:]),
        (beyond & 7) >> 1,
    )
    up, down = jnp.zeros(lane.shape, jnp.float32), jnp.zeros(lane.shape, jnp.float32)
    for b in range(bands):
        begin = 8 * LEVELS * b
        picked = v[begin : begin + 8]
        for k in range(1, LEVELS):
            picked = jnp.where(level_of == k, v[begin + 8 * k : begin + 8 * k + 8], picked)
        vown[b] = picked
        up = jnp.where((row >= 2 * b) & (row < 2 * b + 2), pltpu.roll(picked, 2 * b, 0), up)
        down = jnp.where(row == b, pltpu.roll(picked, b + 3, 0), down)
    vsend_up[...] = up
    vsend_down[...] = down

    expected = (
        (has_low_row & jnp.logical_not(far_low), has_high_row & jnp.logical_not(far_high))
        + (hears_low, hears_high, has_low_col, has_high_col, sends_diagonal & has_low_row, sends_diagonal & has_high_row)
    )
    pl.semaphore_wait(barrier, sum(has.astype(jnp.int32) for has in expected))
    for has, step in ((hears_high, 1), (hears_low, -1)):

        @pl.when(has)
        def _(step=step):
            pl.semaphore_signal(
                told, inc=1, device_id={"row": lax.axis_index("row") + step}, device_id_type=MESH
            )

    def exchange(axis, has_low, has_high, up, down, from_low, from_high, sem):
        here = lax.axis_index(axis)
        to_high = pltpu.make_async_remote_copy(
            up, from_low, sem.at[0], sem.at[1], device_id={axis: here + 1}, device_id_type=MESH
        )
        to_low = pltpu.make_async_remote_copy(
            down, from_high, sem.at[2], sem.at[3], device_id={axis: here - 1}, device_id_type=MESH
        )
        def arrive():
            pl.when(has_low)(to_high.wait_recv)
            pl.when(has_high)(to_low.wait_recv)

        def sent():
            pl.when(has_high)(to_high.wait_send)
            pl.when(has_low)(to_low.wait_send)

        return to_high, to_low, arrive, sent

    v_high, v_low, v_arrive, v_sent = exchange(
        "col", has_low_col, has_high_col, vsend_up, vsend_down, vfrom_low, vfrom_high, v_sem
    )
    pl.when(has_low_col)(v_low.start)
    pl.when(has_high_col)(v_high.start)
    diagonals = []
    for n, (has, step, target) in enumerate(((has_high_row, 1, dfrom_low), (has_low_row, -1, dfrom_high))):
        diagonals.append(
            pltpu.make_async_remote_copy(
                vsend_down.at[:, height:], target, d_sem.at[2 * n], d_sem.at[2 * n + 1],
                device_id={"row": r + step, "col": c - 1}, device_id_type=MESH,
            )
        )
        pl.when(sends_diagonal & has)(diagonals[-1].start)

    half = width // 2
    near = lax.broadcasted_iota(jnp.int32, (1, 128), 1)

    def across_middle(out, left, right):
        before = out[0][:, half // 2 - 128 :] + jnp.where(near == 127, 0.0625 * pltpu.roll(right, 127, 1), 0.0)
        after = out[1][:, :128] + jnp.where(
            near == 0, 0.0625 * pltpu.roll(left, 2, 1) + 0.25 * pltpu.roll(left, 1, 1), 0.0
        )
        return jnp.concatenate([out[0][:, : half // 2 - 128], before], 1), jnp.concatenate(
            [after, out[1][:, 128:]], 1
        )

    for copy in row_loads:
        copy.wait()
    spilled = []
    for b in range(bands):
        high, low = split(strip[b])
        z = dot(rt[...], jnp.concatenate([high, low, high], 0))
        for i in range(tiles):
            zown[b, i] = z[16:32, 128 * i : 128 * i + 128]
        spilled.append(z[0:16])
    spilled = jnp.concatenate(spilled, 0)
    count = spilled.shape[0]
    high, low = split(spilled)
    one = dot(
        jnp.concatenate([high[:, :half], low[:, :half], high[:, half:], low[:, half:]], 0), c1[...]
    )
    one = across_middle(
        (one[:count] + one[count : 2 * count], one[2 * count : 3 * count] + one[3 * count :]),
        spilled[:, half - 128 : half],
        spilled[:, half : half + 128],
    )
    two = dot(jnp.concatenate([high, low], 0), c12[...])
    two = two[:count] + two[count:]
    three = dot_split(two, c3[...])
    four = dot_split(three, c4[...])
    for b in range(bands):
        for side, target in enumerate((zsend_up, zsend_down)):
            g = slice(16 * b + 8 * side, 16 * b + 8 * side + 8)
            pad = jnp.zeros((8, width // 4 - 128), jnp.float32)
            group = lax.broadcasted_iota(jnp.int32, (8, width // 4), 0)
            packed = jnp.where(group < 6, jnp.concatenate([three[g], pad], 1), jnp.concatenate([four[g], pad], 1))
            packed = jnp.where(group < 4, two[g], packed)
            packed = jnp.where(group == 1, pltpu.roll(one[1][g], 1, 0), packed)
            target[b] = jnp.where(group == 0, one[0][g], packed)
    pl.when(far_high | far_low)(lambda: pl.semaphore_wait(told, 1))
    z_high, z_low, z_arrive, z_sent = exchange(
        "row", has_low_row, has_high_row, zsend_up, zsend_down, zfrom_low, zfrom_high, z_sem
    )
    pl.when(has_high_row)(z_high.start)
    pl.when(has_low_row)(z_low.start)

    e_high, e_low, e_arrive, e_sent = exchange(
        "row", has_low_row, has_high_row, esend, esend, efrom_low, efrom_high, e_sem
    )

    def forward(with_high=True):
        pl.when(has_low_col)(v_high.wait_recv)
        low = jnp.where(has_low_col, vfrom_low[...], 0.0)
        if with_high:
            pl.when(has_high_col)(v_low.wait_recv)
            high = jnp.where(has_high_col, vfrom_high[...], 0.0)
        for b in range(bands):
            own = vown[b]
            first = pltpu.roll(own, 6, 0) + pltpu.roll(low, (8 - 2 * b) % 8, 0)
            last = pltpu.roll(own, 3, 0)
            if with_high:
                last = last + pltpu.roll(high, 7 - b, 0)
            both = jnp.where(row < 2, first, jnp.where(row == 7, last, 0.0))
            vown[b] = both
            esend[b] = both[:, height:]
        pl.when(has_high_row)(e_high.start)
        pl.when(has_low_row)(e_low.start)

    def reduce_band(b):
        if b == FORWARD:
            pl.when(direct)(lambda: forward(False))
        if b == EARLY:
            pl.when(late)(forward)
        def reduce_tile(i, carry):
            for source, target in zip(fields[:LEVELS], ys):
                size = target.shape[2] - 2 * PAD
                tap = [source[b, i, pl.ds(PAD - 2 + t, size, stride=2)] for t in range(5)]
                target[b, i, PAD : PAD + size] = (
                    0.0625 * (tap[0] + tap[4]) + 0.25 * (tap[1] + tap[3]) + 0.375 * tap[2]
                )
            for k, y in enumerate(ys):
                y[b, i, PAD : PAD + 2] = y[b, i, PAD : PAD + 2] + zown[b, i, 2 * k : 2 * k + 2]
                end = slice(PAD + sizes[k] - 1, PAD + sizes[k])
                y[b, i, end] = y[b, i, end] + zown[b, i, 8 + 2 * k : 9 + 2 * k]
            return carry

        lax.fori_loop(0, tiles, reduce_tile, 0, unroll=UNROLL)

    late = c >= middle
    inner = x.at[:, 1 : tiles - 1, PAD : PAD + height]
    pltpu.make_async_copy(inner, inner, x_sem.at[2]).wait()
    for b in range(bands):
        reduce_band(b)
    pl.when(jnp.logical_not(late | direct))(forward)

    rest = sum(sizes[1:])
    at = lax.broadcasted_iota(jnp.int32, (128, 128), 1)

    def reduce_columns(b):
        base = 0
        for k in range(LEVELS):
            for i in range(tiles):
                high, low = split(ys[k][b, i, PAD : PAD + sizes[k]])
                if k == 0:
                    h, lanes = divmod(128 * i, half)
                    s1[2 * h * sizes[0] : (2 * h + 1) * sizes[0], lanes : lanes + 128] = high
                    s1[(2 * h + 1) * sizes[0] : (2 * h + 2) * sizes[0], lanes : lanes + 128] = low
                else:
                    s234[base : base + sizes[k], 128 * i : 128 * i + 128] = high
                    s234[rest + base : rest + base + sizes[k], 128 * i : 128 * i + 128] = low
            base += sizes[k] if k else 0
        one = dot(s1[...], c1[...])
        size = sizes[0]
        one = across_middle(
            (one[:size] + one[size : 2 * size], one[2 * size : 3 * size] + one[3 * size :]),
            y1[b, tiles // 2 - 1, PAD : PAD + size],
            y1[b, tiles // 2, PAD : PAD + size],
        )
        o1[b, :, : half // 2] = one[0]
        o1[b, :, half // 2 :] = one[1]
        two = dot(s234[...], c12[...])
        two = two[:rest] + two[rest:]
        three = dot_split(two[sizes[1] :], c3[...])
        four = dot_split(three[sizes[2] :], c4[...])
        o2[b] = two[: sizes[1]]
        o3[b] = three[: sizes[2]]
        o4[b] = four[:, : width >> 4]
    for b in range(bands):
        reduce_columns(b)

    @pl.when(direct)
    def _():
        v_low.wait_recv()
        for b in range(bands):
            vown[b] = vown[b] + jnp.where(row == 7, pltpu.roll(vfrom_high[...], 7 - b, 0), 0.0)

    def finish_columns(b):
        for part, levels in ((0, (0,)), (1, (1, 2, 3))):
            square = jnp.concatenate(
                [vown[b, :, 128 * part : 128 * part + 128], jnp.zeros((120, 128), jnp.float32)], 0
            ).T
            for k in levels:
                out = (o1, o2, o3, o4)[k]
                begin = starts[k] - 128 * part
                value = square[begin : begin + sizes[k]]
                tile = min(out.shape[2], 128)
                mark = at[: sizes[k]]
                low_cells = jnp.where(mark < 2, value, 0.0)[:, :tile]
                high_cells = jnp.where(mark == tile - 1, pltpu.roll(value, tile - 8, 1), 0.0)[:, :tile]
                out[b, :, 0:tile] = out[b, :, 0:tile] + low_cells
                out[b, :, out.shape[2] - tile :] = out[b, :, out.shape[2] - tile :] + high_cells
    for b in range(bands):
        finish_columns(b)

    above = lax.broadcasted_iota(jnp.int32, (8, 128), 1) < 8
    z_arrive()
    for b in range(bands):
        low_rows[b] = jnp.where(has_low_row, zfrom_low[b], 0.0)
        high_rows[b] = jnp.where(has_high_row, zfrom_high[b], 0.0)
    e_arrive()
    from_low, from_high = direct & has_low_row, direct & has_high_row
    pl.when(from_low)(diagonals[0].wait_recv)
    pl.when(from_high)(diagonals[1].wait_recv)
    diagonal = jnp.where(
        above, jnp.where(from_low, dfrom_low[...], 0.0), jnp.where(from_high, dfrom_high[...], 0.0)
    )
    last_row = lax.broadcasted_iota(jnp.int32, (8, 128), 0) == 7
    for b in range(bands):
        corners[b] = jnp.where(
            above,
            jnp.where(has_low_row, efrom_low[b], 0.0),
            jnp.where(has_high_row, efrom_high[b], 0.0),
        ) + jnp.where(last_row, pltpu.roll(diagonal, 7 - b, 0), 0.0)
    pl.when(sends_diagonal & has_high_row)(diagonals[0].wait_send)
    pl.when(sends_diagonal & has_low_row)(diagonals[1].wait_send)
    e_sent()
    z_sent()
    v_sent()


def store_kernel(a1, a2, a3, a4, low_rows, high_rows, corners, o1, o2, o3, o4, t1, t2, t3, t4, in_sem, edge_sem):
    bands = a1.shape[0]
    copies = []
    for k, (source, target) in enumerate(((a1, o1), (a2, o2), (a3, o3))):
        inner = slice(8, source.shape[1] - 8)
        copies.append(pltpu.make_async_copy(source.at[:, inner], target.at[:, inner], in_sem.at[k]))
        copies[-1].start()
    lane = lax.broadcasted_iota(jnp.int32, (16, 128), 1)
    for b in range(bands):
        cells = jnp.concatenate([corners[b], jnp.zeros((120, 128), jnp.float32)], 0).T[:16]
        first = jnp.where(lane < 2, cells, 0.0)
        last = jnp.where(lane == 127, pltpu.roll(cells, 120, 1), 0.0)
        last_half = jnp.where(lane == 63, pltpu.roll(cells, 56, 1), 0.0)
        for side, rows in enumerate((low_rows[b], high_rows[b])):
            for k, (source, target) in enumerate(zip((a1, a2, a3, a4), (t1, t2, t3, t4))):
                size, wide = source.shape[1:]
                count = 2 if side == 0 and k > 0 else 1
                at = slice(8 * side + 2 * k, 8 * side + 2 * k + count)
                if k == 0:
                    none = jnp.zeros((1, wide - 256), jnp.float32)
                    more = jnp.concatenate([rows[0:1], rows[1:2]], 1)
                    more = more + jnp.concatenate([first[at], none, last[at]], 1)
                else:
                    more = rows[2 * k : 2 * k + count, :wide]
                    if k == 1:
                        more = more + jnp.concatenate([first[at], last[at]], 1)
                    elif k == 2:
                        more = more + first[at] + last[at]
                    else:
                        more = more + (first[at] + last_half[at])[:, :wide]
                still = jnp.zeros((8 - count, wide), jnp.float32)
                if side == 0:
                    target[side, b] = source[b, 0:8] + jnp.concatenate([more, still], 0)
                else:
                    target[side, b] = source[b, size - 8 : size] + jnp.concatenate([still, more], 0)
    for k, (source, target) in enumerate(((t1, o1), (t2, o2), (t3, o3), (t4, o4))):
        size = target.shape[1]
        for side, begin in enumerate((0, size - 8)):
            pltpu.make_async_copy(source.at[side], target.at[:, begin : begin + 8], edge_sem.at[k]).start()
        copies.append(pltpu.make_async_copy(source, source, edge_sem.at[k]))
    for copy in copies:
        copy.wait()


def solution(mesh):
    rows_n, cols_n = mesh.shape["row"], mesh.shape["col"]
    row_table, col_table = tables()
    all_rows = whole_rows(256)

    def local(relief):
        bands, height, width = relief.shape
        f32, bf16 = jnp.float32, jnp.bfloat16
        c1 = reduce_matrix(width // 2, False).T
        c12 = chain(width, False)[1].T
        c3 = reduce_matrix(width // 4, False).T
        c4 = np.zeros((width // 4, 128))
        c4[: width // 8, : width // 16] = reduce_matrix(width // 8, False).T
        cc = np.concatenate([c12, c1, np.concatenate([c3, c4], 1)], 0)
        consts = [jnp.asarray(a, bf16) for a in (row_table, col_table, all_rows, cc)]
        shapes = [(bands, height >> k, width >> k) for k in range(1, LEVELS + 1)]

        vmem = lambda *shape, dtype=f32: pltpu.VMEM(shape, dtype)
        scratch = [vmem(bands, 2 * ROW_STRIP, width)]
        scratch += [vmem(bands, width // 128, (height >> k) + 2 * PAD, 128) for k in range(LEVELS + 1)]
        rest = sum(height >> k for k in range(2, LEVELS + 1))
        scratch += [
            vmem(2 * height, width // 2, dtype=bf16), vmem(2 * rest, width, dtype=bf16),
        ]
        scratch += [vmem(*a.shape, dtype=bf16) for a in (row_table[0], col_table[0], all_rows[0], cc)]
        scratch += [vmem(bands, width // 128, 16, 128)]
        scratch += [vmem(bands, 8, width // 4)] * 4
        scratch += [vmem(bands, 8, 128)] * 3
        scratch += [vmem(bands, 8, height + 128)] + [vmem(8, height + 128)] * 4
        scratch += [vmem(8, 128)] * 2
        scratch += [
            pltpu.SemaphoreType.DMA(n) for n in ((2,), (3,), (4,), (4,), (4,), (4,), (4,))
        ]
        scratch += [pltpu.SemaphoreType.REGULAR]
        extra = [(bands, 8, width // 4)] * 2 + [(bands, 8, 128)]
        held = pl.pallas_call(
            functools.partial(pyramid_kernel, rows_n, cols_n),
            out_shape=[jax.ShapeDtypeStruct(s, f32) for s in shapes + extra],
            in_specs=[pl.BlockSpec(memory_space=pltpu.HBM)] * 5,
            out_specs=[pl.BlockSpec(memory_space=pltpu.VMEM)] * (LEVELS + 3),
            scratch_shapes=scratch,
            compiler_params=pltpu.CompilerParams(
                collective_id=0, has_side_effects=True, vmem_limit_bytes=40 << 20
            ),
            name="pyramid",
        )(*[pltpu.with_memory_space_constraint(a, pltpu.HBM) for a in (relief, *consts)])
        return pl.pallas_call(
            store_kernel,
            out_shape=[jax.ShapeDtypeStruct(s, f32) for s in shapes],
            in_specs=[pl.BlockSpec(memory_space=pltpu.VMEM)] * (LEVELS + 3),
            out_specs=[pl.BlockSpec(memory_space=pltpu.HBM)] * LEVELS,
            scratch_shapes=[vmem(2, bands, 8, across) for _, _, across in shapes]
            + [pltpu.SemaphoreType.DMA((LEVELS - 1,)), pltpu.SemaphoreType.DMA((LEVELS,))],
            compiler_params=pltpu.CompilerParams(vmem_limit_bytes=16 << 20),
            name="store",
        )(*held)

    spec = P(None, "row", "col")
    return jax.shard_map(local, mesh=mesh, in_specs=(spec,), out_specs=(spec,) * LEVELS, check_vma=False)
```

```python
import functools

import jax
import jax.numpy as jnp
import numpy as np
from jax import lax
from jax.experimental import pallas as pl
from jax.experimental.pallas import tpu as pltpu
from jax.sharding import PartitionSpec as P

MESH = pl.DeviceIdType.MESH
BINOMIAL = np.array([1, 4, 6, 4, 1]) / 16
LEVELS = 4
PAD = 8
ROW_STRIP = 32
COL_STRIP = 64
UNROLL = 4
DIRECT = 4
FORWARD = 1
EARLY = 1


def reduce_matrix(n, reflect):
    d = np.zeros((n // 2, n))
    for i in range(n // 2):
        for t in range(5):
            c = 2 * i - 2 + t
            if c < 0 or c >= n:
                if not reflect:
                    continue
                c = -c if c < 0 else 2 * (n - 1) - c
            d[i, c] += BINOMIAL[t]
    return d


def chain(n, reflect):
    out, m = [], np.eye(n)
    for _ in range(LEVELS):
        m = reduce_matrix(m.shape[0], reflect) @ m
        out.append(m)
    return out


def edge_parts(n):
    whole, alone = chain(3 * n, True), chain(n, False)
    places = []
    for p in range(3):
        parts = []
        for k in range(LEVELS):
            m = n >> (k + 1)
            mine = whole[k][:, p * n : (p + 1) * n]
            own = mine[p * m : (p + 1) * m] - alone[k]
            assert not own[2:-1].any()
            up = mine[(p + 1) * m : (p + 1) * m + 2] if p < 2 else np.zeros((2, n))
            down = mine[p * m - 1 : p * m] if p > 0 else np.zeros((1, n))
            parts.append((up, down, own[:2], own[-1:]))
        places.append(parts)
    return places


def ends(rows, strip):
    return np.concatenate([rows[:, :strip], rows[:, -strip:]], 1)


def parts_of(table):
    high = np.asarray(jnp.asarray(table, jnp.bfloat16), np.float32)
    return high, table - high


def tables():
    places = edge_parts(256)
    row_table = np.zeros((3, 32, 2 * ROW_STRIP), np.float32)
    col_table = np.zeros((3, 8 * LEVELS, 2 * COL_STRIP), np.float32)
    for p, parts in enumerate(places):
        for k, (up, down, first, last) in enumerate(parts):
            row_table[p, 2 * k : 2 * k + 2] = ends(up, ROW_STRIP)
            row_table[p, 8 + 2 * k] = ends(down, ROW_STRIP)[0]
            row_table[p, 16 + 2 * k : 18 + 2 * k] = ends(first, ROW_STRIP)
            row_table[p, 24 + 2 * k] = ends(last, ROW_STRIP)[0]
            col_table[p, 8 * k : 8 * k + 6] = ends(np.concatenate([up, first, last, down]), COL_STRIP)
    high, low = parts_of(row_table)
    row_table = np.concatenate([high, high, low], 2)
    high, low = parts_of(col_table)
    none = np.zeros_like(low)
    col_table = np.concatenate(
        [np.concatenate([high, high], 2), np.concatenate([low, none], 2)], 1
    )
    return row_table, col_table


ABOVE = ((0, 1), (2, 3), (4, 5), (6, 7))
BELOW = (8, 10, 12, 14)


def whole_rows(n):
    whole = chain(3 * n, True)
    table = np.zeros((3, n, n + 128), np.float32)
    for p in range(3):
        for k in range(LEVELS):
            m, begin = n >> (k + 1), n - (n >> k)
            mine = whole[k][:, p * n : (p + 1) * n]
            table[p, :, begin : begin + m] = mine[p * m : (p + 1) * m].T
            if p < 2:
                for lane, cells in zip(ABOVE[k], mine[(p + 1) * m :]):
                    table[p, :, n + lane] = cells
            if p > 0:
                table[p, :, n + BELOW[k]] = mine[p * m - 1]
    return np.stack(parts_of(table), 1)


def split(a):
    high = a.astype(jnp.bfloat16)
    return high, (a - high.astype(jnp.float32)).astype(jnp.bfloat16)


dot = functools.partial(jnp.dot, preferred_element_type=jnp.float32)


def dot_split(a, weights):
    high, low = split(a)
    return dot(high, weights) + dot(low, weights)


def place(index, count):
    return jnp.where(index == 0, 0, jnp.where(index == count - 1, 2, 1))


def pyramid_kernel(
    rows_n, cols_n, x_hbm, rt_hbm, ct_hbm, wr_hbm, cc_hbm,
    o1, o2, o3, o4, low_rows, high_rows, corners,
    strip, x, y1, y2, y3, y4, s1, s234, rt, ct, wr, cc, zown,
    zsend_up, zsend_down, zfrom_low, zfrom_high,
    esend, efrom_low, efrom_high,
    vown, vsend_up, vsend_down, vfrom_low, vfrom_high, dfrom_low, dfrom_high,
    s_sem, x_sem, t_sem, e_sem, z_sem, v_sem, d_sem, told,
):
    bands, height, width = x_hbm.shape
    tiles = width // 128
    r, c = lax.axis_index("row"), lax.axis_index("col")
    has_low_row, has_high_row = r > 0, r < rows_n - 1
    has_low_col, has_high_col = c > 0, c < cols_n - 1
    ys = (y1, y2, y3, y4)
    fields = (x,) + ys
    sizes = [height >> (k + 1) for k in range(LEVELS)]
    starts = [height - (height >> k) for k in range(LEVELS)]

    def load(source, target, sem):
        copy = pltpu.make_async_copy(source, target, sem)
        copy.start()
        return copy

    def load_tile(i, sem):
        return load(x_hbm.at[:, :, 128 * i : 128 * i + 128], x.at[:, i, PAD : PAD + height], sem)

    col_loads = [
        load(ct_hbm.at[place(c, cols_n)], ct, t_sem.at[0]),
        load_tile(0, x_sem.at[0]),
        load_tile(tiles - 1, x_sem.at[1]),
    ]
    wr_load = load(wr_hbm.at[place(r, rows_n)], wr, t_sem.at[1])

    place_in_line = r % 8
    far_high = (place_in_line == 7) & has_high_row
    far_low = (place_in_line == 0) & has_low_row
    hears_high = (place_in_line == 6) & (r + 2 < rows_n)
    hears_low = (place_in_line == 1) & (r > 1)
    middle = cols_n // 2
    direct = (c >= middle - DIRECT) & (c < middle) & has_high_col
    sends_diagonal = (c > middle - DIRECT) & (c <= middle) & has_low_col
    barrier = pltpu.get_barrier_semaphore()
    for axis, has, step in (
        ("row", has_low_row & jnp.logical_not(far_low), -1), ("row", has_high_row & jnp.logical_not(far_high), 1),
        ("row", far_low, -2), ("row", far_high, 2),
        ("col", has_low_col, -1), ("col", has_high_col, 1),
    ):

        @pl.when(has)
        def _(axis=axis, step=step):
            pl.semaphore_signal(
                barrier, inc=1, device_id={axis: lax.axis_index(axis) + step}, device_id_type=MESH
            )

    for has, step in ((has_low_row, -1), (has_high_row, 1)):

        @pl.when(has & direct)
        def _(step=step):
            pl.semaphore_signal(barrier, inc=1, device_id={"row": r + step, "col": c + 1}, device_id_type=MESH)

    for field in fields[:LEVELS]:
        size = field.shape[2] - 2 * PAD
        zeros = jnp.zeros((bands, tiles, PAD, 128), jnp.float32)
        field[:, :, 0:PAD] = zeros
        field[:, :, PAD + size :] = zeros

    lower_half = lax.broadcasted_iota(jnp.int32, (1, 128), 1) < 64
    for copy in col_loads:
        copy.wait()
    row_loads = [load(rt_hbm.at[place(r, rows_n)], rt, t_sem.at[2])]
    for e, begin in enumerate((0, height - ROW_STRIP)):
        row_loads.append(
            load(
                x_hbm.at[:, begin : begin + ROW_STRIP],
                strip.at[:, e * ROW_STRIP : (e + 1) * ROW_STRIP],
                s_sem.at[e],
            )
        )
    row_loads.append(load(cc_hbm, cc, t_sem.at[3]))
    for i in range(1, tiles - 1):
        load_tile(i, x_sem.at[2])
    c12, c1 = cc.at[0:width], cc.at[width : width + width // 2]
    tail = width + width // 2
    c3, c4 = cc.at[tail : tail + width // 4, 0:128], cc.at[tail : tail + width // 8, 128:256]
    parts = []
    for b in range(bands):
        parts.append(
            jnp.concatenate(
                split(
                    jnp.where(lower_half, x[b, 0, PAD : PAD + height], x[b, tiles - 1, PAD : PAD + height])
                ),
                1,
            )
        )
    v = lax.dot_general(
        ct[...],
        jnp.concatenate(parts, 0),
        (((1,), (1,)), ((), ())),
        preferred_element_type=jnp.float32,
    )
    v = v[: 8 * LEVELS] + v[8 * LEVELS :]
    raw = [v[:, b * height : (b + 1) * height] for b in range(bands)]
    raw = jnp.concatenate(raw, 0)
    wr_load.wait()
    high, low = split(raw)
    v = dot(jnp.concatenate([high, low], 0), wr[0])
    v = v[: raw.shape[0]] + v[raw.shape[0] :]
    v = jnp.concatenate([v[:, :128], v[:, 128:] + dot(high, wr[1, :, 128:])], 1)
    lane = lax.broadcasted_iota(jnp.int32, (8, height + 128), 1)
    row = lax.broadcasted_iota(jnp.int32, (8, height + 128), 0)
    beyond = lane - height
    level_of = jnp.where(
        lane < height,
        sum((lane >= start).astype(jnp.int32) for start in starts[1:]),
        (beyond & 7) >> 1,
    )
    up, down = jnp.zeros(lane.shape, jnp.float32), jnp.zeros(lane.shape, jnp.float32)
    for b in range(bands):
        begin = 8 * LEVELS * b
        picked = v[begin : begin + 8]
        for k in range(1, LEVELS):
            picked = jnp.where(level_of == k, v[begin + 8 * k : begin + 8 * k + 8], picked)
        vown[b] = picked
        up = jnp.where((row >= 2 * b) & (row < 2 * b + 2), pltpu.roll(picked, 2 * b, 0), up)
        down = jnp.where(row == b, pltpu.roll(picked, b + 3, 0), down)
    vsend_up[...] = up
    vsend_down[...] = down

    expected = (
        (has_low_row & jnp.logical_not(far_low), has_high_row & jnp.logical_not(far_high))
        + (hears_low, hears_high, has_low_col, has_high_col, sends_diagonal & has_low_row, sends_diagonal & has_high_row)
    )
    pl.semaphore_wait(barrier, sum(has.astype(jnp.int32) for has in expected))
    for has, step in ((hears_high, 1), (hears_low, -1)):

        @pl.when(has)
        def _(step=step):
            pl.semaphore_signal(
                told, inc=1, device_id={"row": lax.axis_index("row") + step}, device_id_type=MESH
            )

    def exchange(axis, has_low, has_high, up, down, from_low, from_high, sem):
        here = lax.axis_index(axis)
        to_high = pltpu.make_async_remote_copy(
            up, from_low, sem.at[0], sem.at[1], device_id={axis: here + 1}, device_id_type=MESH
        )
        to_low = pltpu.make_async_remote_copy(
            down, from_high, sem.at[2], sem.at[3], device_id={axis: here - 1}, device_id_type=MESH
        )
        def arrive():
            pl.when(has_low)(to_high.wait_recv)
            pl.when(has_high)(to_low.wait_recv)

        def sent():
            pl.when(has_high)(to_high.wait_send)
            pl.when(has_low)(to_low.wait_send)

        return to_high, to_low, arrive, sent

    v_high, v_low, v_arrive, v_sent = exchange(
        "col", has_low_col, has_high_col, vsend_up, vsend_down, vfrom_low, vfrom_high, v_sem
    )
    pl.when(has_low_col)(v_low.start)
    pl.when(has_high_col)(v_high.start)
    diagonals = []
    for n, (has, step, target) in enumerate(((has_high_row, 1, dfrom_low), (has_low_row, -1, dfrom_high))):
        diagonals.append(
            pltpu.make_async_remote_copy(
                vsend_down.at[:, height:], target, d_sem.at[2 * n], d_sem.at[2 * n + 1],
                device_id={"row": r + step, "col": c - 1}, device_id_type=MESH,
            )
        )
        pl.when(sends_diagonal & has)(diagonals[-1].start)

    half = width // 2
    near = lax.broadcasted_iota(jnp.int32, (1, 128), 1)

    def across_middle(out, left, right):
        before = out[0][:, half // 2 - 128 :] + jnp.where(near == 127, 0.0625 * pltpu.roll(right, 127, 1), 0.0)
        after = out[1][:, :128] + jnp.where(
            near == 0, 0.0625 * pltpu.roll(left, 2, 1) + 0.25 * pltpu.roll(left, 1, 1), 0.0
        )
        return jnp.concatenate([out[0][:, : half // 2 - 128], before], 1), jnp.concatenate(
            [after, out[1][:, 128:]], 1
        )

    for copy in row_loads:
        copy.wait()
    spilled = []
    for b in range(bands):
        high, low = split(strip[b])
        z = dot(rt[...], jnp.concatenate([high, low, high], 0))
        for i in range(tiles):
            zown[b, i] = z[16:32, 128 * i : 128 * i + 128]
        spilled.append(z[0:16])
    spilled = jnp.concatenate(spilled, 0)
    count = spilled.shape[0]
    high, low = split(spilled)
    one = dot(
        jnp.concatenate([high[:, :half], low[:, :half], high[:, half:], low[:, half:]], 0), c1[...]
    )
    one = across_middle(
        (one[:count] + one[count : 2 * count], one[2 * count : 3 * count] + one[3 * count :]),
        spilled[:, half - 128 : half],
        spilled[:, half : half + 128],
    )
    two = dot(jnp.concatenate([high, low], 0), c12[...])
    two = two[:count] + two[count:]
    three = dot_split(two, c3[...])
    four = dot_split(three, c4[...])
    for b in range(bands):
        for side, target in enumerate((zsend_up, zsend_down)):
            g = slice(16 * b + 8 * side, 16 * b + 8 * side + 8)
            pad = jnp.zeros((8, width // 4 - 128), jnp.float32)
            group = lax.broadcasted_iota(jnp.int32, (8, width // 4), 0)
            packed = jnp.where(group < 6, jnp.concatenate([three[g], pad], 1), jnp.concatenate([four[g], pad], 1))
            packed = jnp.where(group < 4, two[g], packed)
            packed = jnp.where(group == 1, pltpu.roll(one[1][g], 1, 0), packed)
            target[b] = jnp.where(group == 0, one[0][g], packed)
    pl.when(far_high | far_low)(lambda: pl.semaphore_wait(told, 1))
    z_high, z_low, z_arrive, z_sent = exchange(
        "row", has_low_row, has_high_row, zsend_up, zsend_down, zfrom_low, zfrom_high, z_sem
    )
    pl.when(has_high_row)(z_high.start)
    pl.when(has_low_row)(z_low.start)

    e_high, e_low, e_arrive, e_sent = exchange(
        "row", has_low_row, has_high_row, esend, esend, efrom_low, efrom_high, e_sem
    )

    def forward(with_high=True):
        pl.when(has_low_col)(v_high.wait_recv)
        low = jnp.where(has_low_col, vfrom_low[...], 0.0)
        if with_high:
            pl.when(has_high_col)(v_low.wait_recv)
            high = jnp.where(has_high_col, vfrom_high[...], 0.0)
        for b in range(bands):
            own = vown[b]
            first = pltpu.roll(own, 6, 0) + pltpu.roll(low, (8 - 2 * b) % 8, 0)
            last = pltpu.roll(own, 3, 0)
            if with_high:
                last = last + pltpu.roll(high, 7 - b, 0)
            both = jnp.where(row < 2, first, jnp.where(row == 7, last, 0.0))
            vown[b] = both
            esend[b] = both[:, height:]
        pl.when(has_high_row)(e_high.start)
        pl.when(has_low_row)(e_low.start)

    def reduce_band(b):
        if b == FORWARD:
            pl.when(direct & jnp.logical_not(after_last))(lambda: forward(False))
        if b == bands - 1:
            pl.when(direct & after_last)(lambda: forward(False))
        if b == EARLY:
            pl.when(late)(forward)
        def reduce_tile(i, carry):
            for source, target in zip(fields[:LEVELS], ys):
                size = target.shape[2] - 2 * PAD
                tap = [source[b, i, pl.ds(PAD - 2 + t, size, stride=2)] for t in range(5)]
                target[b, i, PAD : PAD + size] = (
                    0.0625 * (tap[0] + tap[4]) + 0.25 * (tap[1] + tap[3]) + 0.375 * tap[2]
                )
            for k, y in enumerate(ys):
                y[b, i, PAD : PAD + 2] = y[b, i, PAD : PAD + 2] + zown[b, i, 2 * k : 2 * k + 2]
                end = slice(PAD + sizes[k] - 1, PAD + sizes[k])
                y[b, i, end] = y[b, i, end] + zown[b, i, 8 + 2 * k : 9 + 2 * k]
            return carry

        lax.fori_loop(0, tiles, reduce_tile, 0, unroll=UNROLL)

    late = c >= middle
    after_last = (r == 0) & (c == 1)
    inner = x.at[:, 1 : tiles - 1, PAD : PAD + height]
    pltpu.make_async_copy(inner, inner, x_sem.at[2]).wait()
    for b in range(bands):
        reduce_band(b)
    pl.when(jnp.logical_not(late | direct))(forward)

    rest = sum(sizes[1:])
    at = lax.broadcasted_iota(jnp.int32, (128, 128), 1)

    def reduce_columns(b):
        base = 0
        for k in range(LEVELS):
            for i in range(tiles):
                high, low = split(ys[k][b, i, PAD : PAD + sizes[k]])
                if k == 0:
                    h, lanes = divmod(128 * i, half)
                    s1[2 * h * sizes[0] : (2 * h + 1) * sizes[0], lanes : lanes + 128] = high
                    s1[(2 * h + 1) * sizes[0] : (2 * h + 2) * sizes[0], lanes : lanes + 128] = low
                else:
                    s234[base : base + sizes[k], 128 * i : 128 * i + 128] = high
                    s234[rest + base : rest + base + sizes[k], 128 * i : 128 * i + 128] = low
            base += sizes[k] if k else 0
        one = dot(s1[...], c1[...])
        size = sizes[0]
        one = across_middle(
            (one[:size] + one[size : 2 * size], one[2 * size : 3 * size] + one[3 * size :]),
            y1[b, tiles // 2 - 1, PAD : PAD + size],
            y1[b, tiles // 2, PAD : PAD + size],
        )
        o1[b, :, : half // 2] = one[0]
        o1[b, :, half // 2 :] = one[1]
        two = dot(s234[...], c12[...])
        two = two[:rest] + two[rest:]
        three = dot_split(two[sizes[1] :], c3[...])
        four = dot_split(three[sizes[2] :], c4[...])
        o2[b] = two[: sizes[1]]
        o3[b] = three[: sizes[2]]
        o4[b] = four[:, : width >> 4]
    for b in range(bands):
        reduce_columns(b)

    @pl.when(direct)
    def _():
        v_low.wait_recv()
        for b in range(bands):
            vown[b] = vown[b] + jnp.where(row == 7, pltpu.roll(vfrom_high[...], 7 - b, 0), 0.0)

    def finish_columns(b):
        for part, levels in ((0, (0,)), (1, (1, 2, 3))):
            square = jnp.concatenate(
                [vown[b, :, 128 * part : 128 * part + 128], jnp.zeros((120, 128), jnp.float32)], 0
            ).T
            for k in levels:
                out = (o1, o2, o3, o4)[k]
                begin = starts[k] - 128 * part
                value = square[begin : begin + sizes[k]]
                tile = min(out.shape[2], 128)
                mark = at[: sizes[k]]
                low_cells = jnp.where(mark < 2, value, 0.0)[:, :tile]
                high_cells = jnp.where(mark == tile - 1, pltpu.roll(value, tile - 8, 1), 0.0)[:, :tile]
                out[b, :, 0:tile] = out[b, :, 0:tile] + low_cells
                out[b, :, out.shape[2] - tile :] = out[b, :, out.shape[2] - tile :] + high_cells
    for b in range(bands):
        finish_columns(b)

    above = lax.broadcasted_iota(jnp.int32, (8, 128), 1) < 8
    z_arrive()
    for b in range(bands):
        low_rows[b] = jnp.where(has_low_row, zfrom_low[b], 0.0)
        high_rows[b] = jnp.where(has_high_row, zfrom_high[b], 0.0)
    e_arrive()
    from_low, from_high = direct & has_low_row, direct & has_high_row
    pl.when(from_low)(diagonals[0].wait_recv)
    pl.when(from_high)(diagonals[1].wait_recv)
    diagonal = jnp.where(
        above, jnp.where(from_low, dfrom_low[...], 0.0), jnp.where(from_high, dfrom_high[...], 0.0)
    )
    last_row = lax.broadcasted_iota(jnp.int32, (8, 128), 0) == 7
    for b in range(bands):
        corners[b] = jnp.where(
            above,
            jnp.where(has_low_row, efrom_low[b], 0.0),
            jnp.where(has_high_row, efrom_high[b], 0.0),
        ) + jnp.where(last_row, pltpu.roll(diagonal, 7 - b, 0), 0.0)
    pl.when(sends_diagonal & has_high_row)(diagonals[0].wait_send)
    pl.when(sends_diagonal & has_low_row)(diagonals[1].wait_send)
    e_sent()
    z_sent()
    v_sent()


def store_kernel(a1, a2, a3, a4, low_rows, high_rows, corners, o1, o2, o3, o4, t1, t2, t3, t4, in_sem, edge_sem):
    bands = a1.shape[0]
    copies = []
    for k, (source, target) in enumerate(((a1, o1), (a2, o2), (a3, o3))):
        inner = slice(8, source.shape[1] - 8)
        copies.append(pltpu.make_async_copy(source.at[:, inner], target.at[:, inner], in_sem.at[k]))
        copies[-1].start()
    lane = lax.broadcasted_iota(jnp.int32, (16, 128), 1)
    for b in range(bands):
        cells = jnp.concatenate([corners[b], jnp.zeros((120, 128), jnp.float32)], 0).T[:16]
        first = jnp.where(lane < 2, cells, 0.0)
        last = jnp.where(lane == 127, pltpu.roll(cells, 120, 1), 0.0)
        last_half = jnp.where(lane == 63, pltpu.roll(cells, 56, 1), 0.0)
        for side, rows in enumerate((low_rows[b], high_rows[b])):
            for k, (source, target) in enumerate(zip((a1, a2, a3, a4), (t1, t2, t3, t4))):
                size, wide = source.shape[1:]
                count = 2 if side == 0 and k > 0 else 1
                at = slice(8 * side + 2 * k, 8 * side + 2 * k + count)
                if k == 0:
                    none = jnp.zeros((1, wide - 256), jnp.float32)
                    more = jnp.concatenate([rows[0:1], rows[1:2]], 1)
                    more = more + jnp.concatenate([first[at], none, last[at]], 1)
                else:
                    more = rows[2 * k : 2 * k + count, :wide]
                    if k == 1:
                        more = more + jnp.concatenate([first[at], last[at]], 1)
                    elif k == 2:
                        more = more + first[at] + last[at]
                    else:
                        more = more + (first[at] + last_half[at])[:, :wide]
                still = jnp.zeros((8 - count, wide), jnp.float32)
                if side == 0:
                    target[side, b] = source[b, 0:8] + jnp.concatenate([more, still], 0)
                else:
                    target[side, b] = source[b, size - 8 : size] + jnp.concatenate([still, more], 0)
    for k, (source, target) in enumerate(((t1, o1), (t2, o2), (t3, o3), (t4, o4))):
        size = target.shape[1]
        for side, begin in enumerate((0, size - 8)):
            pltpu.make_async_copy(source.at[side], target.at[:, begin : begin + 8], edge_sem.at[k]).start()
        copies.append(pltpu.make_async_copy(source, source, edge_sem.at[k]))
    for copy in copies:
        copy.wait()


def solution(mesh):
    rows_n, cols_n = mesh.shape["row"], mesh.shape["col"]
    row_table, col_table = tables()
    all_rows = whole_rows(256)

    def local(relief):
        bands, height, width = relief.shape
        f32, bf16 = jnp.float32, jnp.bfloat16
        c1 = reduce_matrix(width // 2, False).T
        c12 = chain(width, False)[1].T
        c3 = reduce_matrix(width // 4, False).T
        c4 = np.zeros((width // 4, 128))
        c4[: width // 8, : width // 16] = reduce_matrix(width // 8, False).T
        cc = np.concatenate([c12, c1, np.concatenate([c3, c4], 1)], 0)
        consts = [jnp.asarray(a, bf16) for a in (row_table, col_table, all_rows, cc)]
        shapes = [(bands, height >> k, width >> k) for k in range(1, LEVELS + 1)]

        vmem = lambda *shape, dtype=f32: pltpu.VMEM(shape, dtype)
        scratch = [vmem(bands, 2 * ROW_STRIP, width)]
        scratch += [vmem(bands, width // 128, (height >> k) + 2 * PAD, 128) for k in range(LEVELS + 1)]
        rest = sum(height >> k for k in range(2, LEVELS + 1))
        scratch += [
            vmem(2 * height, width // 2, dtype=bf16), vmem(2 * rest, width, dtype=bf16),
        ]
        scratch += [vmem(*a.shape, dtype=bf16) for a in (row_table[0], col_table[0], all_rows[0], cc)]
        scratch += [vmem(bands, width // 128, 16, 128)]
        scratch += [vmem(bands, 8, width // 4)] * 4
        scratch += [vmem(bands, 8, 128)] * 3
        scratch += [vmem(bands, 8, height + 128)] + [vmem(8, height + 128)] * 4
        scratch += [vmem(8, 128)] * 2
        scratch += [
            pltpu.SemaphoreType.DMA(n) for n in ((2,), (3,), (4,), (4,), (4,), (4,), (4,))
        ]
        scratch += [pltpu.SemaphoreType.REGULAR]
        extra = [(bands, 8, width // 4)] * 2 + [(bands, 8, 128)]
        held = pl.pallas_call(
            functools.partial(pyramid_kernel, rows_n, cols_n),
            out_shape=[jax.ShapeDtypeStruct(s, f32) for s in shapes + extra],
            in_specs=[pl.BlockSpec(memory_space=pltpu.HBM)] * 5,
            out_specs=[pl.BlockSpec(memory_space=pltpu.VMEM)] * (LEVELS + 3),
            scratch_shapes=scratch,
            compiler_params=pltpu.CompilerParams(
                collective_id=0, has_side_effects=True, vmem_limit_bytes=40 << 20
            ),
            name="pyramid",
        )(*[pltpu.with_memory_space_constraint(a, pltpu.HBM) for a in (relief, *consts)])
        return pl.pallas_call(
            store_kernel,
            out_shape=[jax.ShapeDtypeStruct(s, f32) for s in shapes],
            in_specs=[pl.BlockSpec(memory_space=pltpu.VMEM)] * (LEVELS + 3),
            out_specs=[pl.BlockSpec(memory_space=pltpu.HBM)] * LEVELS,
            scratch_shapes=[vmem(2, bands, 8, across) for _, _, across in shapes]
            + [pltpu.SemaphoreType.DMA((LEVELS - 1,)), pltpu.SemaphoreType.DMA((LEVELS,))],
            compiler_params=pltpu.CompilerParams(vmem_limit_bytes=16 << 20),
            name="store",
        )(*held)

    spec = P(None, "row", "col")
    return jax.shard_map(local, mesh=mesh, in_specs=(spec,), out_specs=(spec,) * LEVELS, check_vma=False)
```

```python
import functools

import jax
import jax.numpy as jnp
import numpy as np
from jax import lax
from jax.experimental import pallas as pl
from jax.experimental.pallas import tpu as pltpu
from jax.sharding import PartitionSpec as P

MESH = pl.DeviceIdType.MESH
BINOMIAL = np.array([1, 4, 6, 4, 1]) / 16
LEVELS = 4
PAD = 8
ROW_STRIP = 32
COL_STRIP = 64
UNROLL = 8
DIRECT = 4
FORWARD = 1
EARLY = 1


def reduce_matrix(n, reflect):
    d = np.zeros((n // 2, n))
    for i in range(n // 2):
        for t in range(5):
            c = 2 * i - 2 + t
            if c < 0 or c >= n:
                if not reflect:
                    continue
                c = -c if c < 0 else 2 * (n - 1) - c
            d[i, c] += BINOMIAL[t]
    return d


def chain(n, reflect):
    out, m = [], np.eye(n)
    for _ in range(LEVELS):
        m = reduce_matrix(m.shape[0], reflect) @ m
        out.append(m)
    return out


def edge_parts(n):
    whole, alone = chain(3 * n, True), chain(n, False)
    places = []
    for p in range(3):
        parts = []
        for k in range(LEVELS):
            m = n >> (k + 1)
            mine = whole[k][:, p * n : (p + 1) * n]
            own = mine[p * m : (p + 1) * m] - alone[k]
            assert not own[2:-1].any()
            up = mine[(p + 1) * m : (p + 1) * m + 2] if p < 2 else np.zeros((2, n))
            down = mine[p * m - 1 : p * m] if p > 0 else np.zeros((1, n))
            parts.append((up, down, own[:2], own[-1:]))
        places.append(parts)
    return places


def ends(rows, strip):
    return np.concatenate([rows[:, :strip], rows[:, -strip:]], 1)


def parts_of(table):
    high = np.asarray(jnp.asarray(table, jnp.bfloat16), np.float32)
    return high, table - high


def tables():
    places = edge_parts(256)
    row_table = np.zeros((3, 32, 2 * ROW_STRIP), np.float32)
    col_table = np.zeros((3, 8 * LEVELS, 2 * COL_STRIP), np.float32)
    for p, parts in enumerate(places):
        for k, (up, down, first, last) in enumerate(parts):
            row_table[p, 2 * k : 2 * k + 2] = ends(up, ROW_STRIP)
            row_table[p, 8 + 2 * k] = ends(down, ROW_STRIP)[0]
            row_table[p, 16 + 2 * k : 18 + 2 * k] = ends(first, ROW_STRIP)
            row_table[p, 24 + 2 * k] = ends(last, ROW_STRIP)[0]
            col_table[p, 8 * k : 8 * k + 6] = ends(np.concatenate([up, first, last, down]), COL_STRIP)
    high, low = parts_of(row_table)
    row_table = np.concatenate([high, high, low], 2)
    high, low = parts_of(col_table)
    none = np.zeros_like(low)
    col_table = np.concatenate(
        [np.concatenate([high, high], 2), np.concatenate([low, none], 2)], 1
    )
    return row_table, col_table


ABOVE = ((0, 1), (2, 3), (4, 5), (6, 7))
BELOW = (8, 10, 12, 14)


def whole_rows(n):
    whole = chain(3 * n, True)
    table = np.zeros((3, n, n + 128), np.float32)
    for p in range(3):
        for k in range(LEVELS):
            m, begin = n >> (k + 1), n - (n >> k)
            mine = whole[k][:, p * n : (p + 1) * n]
            table[p, :, begin : begin + m] = mine[p * m : (p + 1) * m].T
            if p < 2:
                for lane, cells in zip(ABOVE[k], mine[(p + 1) * m :]):
                    table[p, :, n + lane] = cells
            if p > 0:
                table[p, :, n + BELOW[k]] = mine[p * m - 1]
    return np.stack(parts_of(table), 1)


def split(a):
    high = a.astype(jnp.bfloat16)
    return high, (a - high.astype(jnp.float32)).astype(jnp.bfloat16)


dot = functools.partial(jnp.dot, preferred_element_type=jnp.float32)


def dot_split(a, weights):
    high, low = split(a)
    return dot(high, weights) + dot(low, weights)


def place(index, count):
    return jnp.where(index == 0, 0, jnp.where(index == count - 1, 2, 1))


def pyramid_kernel(
    rows_n, cols_n, x_hbm, rt_hbm, ct_hbm, wr_hbm, cc_hbm,
    o1, o2, o3, o4, low_rows, high_rows, corners,
    strip, x, y1, y2, y3, y4, s1, s234, rt, ct, wr, cc, zown,
    zsend_up, zsend_down, zfrom_low, zfrom_high,
    esend, efrom_low, efrom_high,
    vown, vsend_up, vsend_down, vfrom_low, vfrom_high, dfrom_low, dfrom_high,
    s_sem, x_sem, t_sem, e_sem, z_sem, v_sem, d_sem, told,
):
    bands, height, width = x_hbm.shape
    tiles = width // 128
    r, c = lax.axis_index("row"), lax.axis_index("col")
    has_low_row, has_high_row = r > 0, r < rows_n - 1
    has_low_col, has_high_col = c > 0, c < cols_n - 1
    ys = (y1, y2, y3, y4)
    fields = (x,) + ys
    sizes = [height >> (k + 1) for k in range(LEVELS)]
    starts = [height - (height >> k) for k in range(LEVELS)]

    def load(source, target, sem):
        copy = pltpu.make_async_copy(source, target, sem)
        copy.start()
        return copy

    def load_tile(i, sem):
        return load(x_hbm.at[:, :, 128 * i : 128 * i + 128], x.at[:, i, PAD : PAD + height], sem)

    col_loads = [
        load_tile(0, x_sem.at[0]),
        load_tile(tiles - 1, x_sem.at[1]),
        load(ct_hbm.at[place(c, cols_n)], ct, t_sem.at[0]),
    ]
    wr_load = load(wr_hbm.at[place(r, rows_n)], wr, t_sem.at[1])

    place_in_line = r % 8
    far_high = (place_in_line == 7) & has_high_row
    far_low = (place_in_line == 0) & has_low_row
    hears_high = (place_in_line == 6) & (r + 2 < rows_n)
    hears_low = (place_in_line == 1) & (r > 1)
    middle = cols_n // 2
    direct = (c >= middle - DIRECT) & (c < middle) & has_high_col
    sends_diagonal = (c > middle - DIRECT) & (c <= middle) & has_low_col
    barrier = pltpu.get_barrier_semaphore()
    for axis, has, step in (
        ("row", has_low_row & jnp.logical_not(far_low), -1), ("row", has_high_row & jnp.logical_not(far_high), 1),
        ("row", far_low, -2), ("row", far_high, 2),
        ("col", has_low_col, -1), ("col", has_high_col, 1),
    ):

        @pl.when(has)
        def _(axis=axis, step=step):
            pl.semaphore_signal(
                barrier, inc=1, device_id={axis: lax.axis_index(axis) + step}, device_id_type=MESH
            )

    for has, step in ((has_low_row, -1), (has_high_row, 1)):

        @pl.when(has & direct)
        def _(step=step):
            pl.semaphore_signal(barrier, inc=1, device_id={"row": r + step, "col": c + 1}, device_id_type=MESH)

    for field in fields[:LEVELS]:
        size = field.shape[2] - 2 * PAD
        zeros = jnp.zeros((bands, tiles, PAD, 128), jnp.float32)
        field[:, :, 0:PAD] = zeros
        field[:, :, PAD + size :] = zeros

    lower_half = lax.broadcasted_iota(jnp.int32, (1, 128), 1) < 64
    for copy in col_loads:
        copy.wait()
    row_loads = [load(rt_hbm.at[place(r, rows_n)], rt, t_sem.at[2])]
    for e, begin in enumerate((0, height - ROW_STRIP)):
        load(
            x_hbm.at[:, begin : begin + ROW_STRIP], strip.at[:, e * ROW_STRIP : (e + 1) * ROW_STRIP], s_sem
        )
    row_loads.append(pltpu.make_async_copy(strip, strip, s_sem))
    row_loads.append(load(cc_hbm, cc, t_sem.at[3]))
    for i in range(1, tiles - 1):
        load_tile(i, x_sem.at[2])
    c12, c1 = cc.at[0:width], cc.at[width : width + width // 2]
    tail = width + width // 2
    c3, c4 = cc.at[tail : tail + width // 4, 0:128], cc.at[tail : tail + width // 8, 128:256]
    parts = []
    for b in range(bands):
        parts.append(
            jnp.concatenate(
                split(
                    jnp.where(lower_half, x[b, 0, PAD : PAD + height], x[b, tiles - 1, PAD : PAD + height])
                ),
                1,
            )
        )
    v = lax.dot_general(
        ct[...],
        jnp.concatenate(parts, 0),
        (((1,), (1,)), ((), ())),
        preferred_element_type=jnp.float32,
    )
    v = v[: 8 * LEVELS] + v[8 * LEVELS :]
    raw = [v[:, b * height : (b + 1) * height] for b in range(bands)]
    raw = jnp.concatenate(raw, 0)
    wr_load.wait()
    high, low = split(raw)
    v = dot(jnp.concatenate([high, low], 0), wr[0])
    v = v[: raw.shape[0]] + v[raw.shape[0] :]
    v = jnp.concatenate([v[:, :128], v[:, 128:] + dot(high, wr[1, :, 128:])], 1)
    lane = lax.broadcasted_iota(jnp.int32, (8, height + 128), 1)
    row = lax.broadcasted_iota(jnp.int32, (8, height + 128), 0)
    beyond = lane - height
    level_of = jnp.where(
        lane < height,
        sum((lane >= start).astype(jnp.int32) for start in starts[1:]),
        (beyond & 7) >> 1,
    )
    up, down = jnp.zeros(lane.shape, jnp.float32), jnp.zeros(lane.shape, jnp.float32)
    for b in range(bands):
        begin = 8 * LEVELS * b
        picked = v[begin : begin + 8]
        for k in range(1, LEVELS):
            picked = jnp.where(level_of == k, v[begin + 8 * k : begin + 8 * k + 8], picked)
        vown[b] = picked
        up = jnp.where((row >= 2 * b) & (row < 2 * b + 2), pltpu.roll(picked, 2 * b, 0), up)
        down = jnp.where(row == b, pltpu.roll(picked, b + 3, 0), down)
    vsend_up[...] = up
    vsend_down[...] = down

    expected = (
        (has_low_row & jnp.logical_not(far_low), has_high_row & jnp.logical_not(far_high))
        + (hears_low, hears_high, has_low_col, has_high_col, sends_diagonal & has_low_row, sends_diagonal & has_high_row)
    )
    pl.semaphore_wait(barrier, sum(has.astype(jnp.int32) for has in expected))
    for has, step in ((hears_high, 1), (hears_low, -1)):

        @pl.when(has)
        def _(step=step):
            pl.semaphore_signal(
                told, inc=1, device_id={"row": lax.axis_index("row") + step}, device_id_type=MESH
            )

    def exchange(axis, has_low, has_high, up, down, from_low, from_high, sem):
        here = lax.axis_index(axis)
        to_high = pltpu.make_async_remote_copy(
            up, from_low, sem.at[0], sem.at[1], device_id={axis: here + 1}, device_id_type=MESH
        )
        to_low = pltpu.make_async_remote_copy(
            down, from_high, sem.at[2], sem.at[3], device_id={axis: here - 1}, device_id_type=MESH
        )
        def arrive():
            pl.when(has_low)(to_high.wait_recv)
            pl.when(has_high)(to_low.wait_recv)

        def sent():
            pl.when(has_high)(to_high.wait_send)
            pl.when(has_low)(to_low.wait_send)

        return to_high, to_low, arrive, sent

    v_high, v_low, v_arrive, v_sent = exchange(
        "col", has_low_col, has_high_col, vsend_up, vsend_down, vfrom_low, vfrom_high, v_sem
    )
    pl.when(has_low_col)(v_low.start)
    pl.when(has_high_col)(v_high.start)
    diagonals = []
    for n, (has, step, target) in enumerate(((has_high_row, 1, dfrom_low), (has_low_row, -1, dfrom_high))):
        diagonals.append(
            pltpu.make_async_remote_copy(
                vsend_down.at[:, height:], target, d_sem.at[2 * n], d_sem.at[2 * n + 1],
                device_id={"row": r + step, "col": c - 1}, device_id_type=MESH,
            )
        )
        pl.when(sends_diagonal & has)(diagonals[-1].start)

    half = width // 2
    near = lax.broadcasted_iota(jnp.int32, (1, 128), 1)

    def across_middle(out, left, right):
        before = out[0][:, half // 2 - 128 :] + jnp.where(near == 127, 0.0625 * pltpu.roll(right, 127, 1), 0.0)
        after = out[1][:, :128] + jnp.where(
            near == 0, 0.0625 * pltpu.roll(left, 2, 1) + 0.25 * pltpu.roll(left, 1, 1), 0.0
        )
        return jnp.concatenate([out[0][:, : half // 2 - 128], before], 1), jnp.concatenate(
            [after, out[1][:, 128:]], 1
        )

    for copy in row_loads:
        copy.wait()
    spilled = []
    for b in range(bands):
        high, low = split(strip[b])
        z = dot(rt[...], jnp.concatenate([high, low, high], 0))
        for i in range(tiles):
            zown[b, i] = z[16:32, 128 * i : 128 * i + 128]
        spilled.append(z[0:16])
    spilled = jnp.concatenate(spilled, 0)
    count = spilled.shape[0]
    high, low = split(spilled)
    one = dot(
        jnp.concatenate([high[:, :half], low[:, :half], high[:, half:], low[:, half:]], 0), c1[...]
    )
    one = across_middle(
        (one[:count] + one[count : 2 * count], one[2 * count : 3 * count] + one[3 * count :]),
        spilled[:, half - 128 : half],
        spilled[:, half : half + 128],
    )
    two = dot(jnp.concatenate([high, low], 0), c12[...])
    two = two[:count] + two[count:]
    three = dot_split(two, c3[...])
    four = dot_split(three, c4[...])
    for b in range(bands):
        for side, target in enumerate((zsend_up, zsend_down)):
            g = slice(16 * b + 8 * side, 16 * b + 8 * side + 8)
            pad = jnp.zeros((8, width // 4 - 128), jnp.float32)
            group = lax.broadcasted_iota(jnp.int32, (8, width // 4), 0)
            packed = jnp.where(group < 6, jnp.concatenate([three[g], pad], 1), jnp.concatenate([four[g], pad], 1))
            packed = jnp.where(group < 4, two[g], packed)
            packed = jnp.where(group == 1, pltpu.roll(one[1][g], 1, 0), packed)
            target[b] = jnp.where(group == 0, one[0][g], packed)
    pl.when(far_high | far_low)(lambda: pl.semaphore_wait(told, 1))
    z_high, z_low, z_arrive, z_sent = exchange(
        "row", has_low_row, has_high_row, zsend_up, zsend_down, zfrom_low, zfrom_high, z_sem
    )
    pl.when(has_high_row)(z_high.start)
    pl.when(has_low_row)(z_low.start)

    e_high, e_low, e_arrive, e_sent = exchange(
        "row", has_low_row, has_high_row, esend, esend, efrom_low, efrom_high, e_sem
    )

    def forward(with_high=True):
        pl.when(has_low_col)(v_high.wait_recv)
        low = jnp.where(has_low_col, vfrom_low[...], 0.0)
        if with_high:
            pl.when(has_high_col)(v_low.wait_recv)
            high = jnp.where(has_high_col, vfrom_high[...], 0.0)
        for b in range(bands):
            own = vown[b]
            first = pltpu.roll(own, 6, 0) + pltpu.roll(low, (8 - 2 * b) % 8, 0)
            last = pltpu.roll(own, 3, 0)
            if with_high:
                last = last + pltpu.roll(high, 7 - b, 0)
            both = jnp.where(row < 2, first, jnp.where(row == 7, last, 0.0))
            vown[b] = both
            esend[b] = both[:, height:]
        pl.when(has_high_row)(e_high.start)
        pl.when(has_low_row)(e_low.start)

    def reduce_band(b):
        if b == FORWARD:
            pl.when(direct & jnp.logical_not(after_last))(lambda: forward(False))
        if b == bands - 1:
            pl.when(direct & after_last)(lambda: forward(False))
        if b == EARLY:
            pl.when(late)(forward)
        def reduce_tile(i, carry):
            for source, target in zip(fields[:LEVELS], ys):
                size = target.shape[2] - 2 * PAD
                tap = [source[b, i, pl.ds(PAD - 2 + t, size, stride=2)] for t in range(5)]
                target[b, i, PAD : PAD + size] = (
                    0.0625 * (tap[0] + tap[4]) + 0.25 * (tap[1] + tap[3]) + 0.375 * tap[2]
                )
            for k, y in enumerate(ys):
                y[b, i, PAD : PAD + 2] = y[b, i, PAD : PAD + 2] + zown[b, i, 2 * k : 2 * k + 2]
                end = slice(PAD + sizes[k] - 1, PAD + sizes[k])
                y[b, i, end] = y[b, i, end] + zown[b, i, 8 + 2 * k : 9 + 2 * k]
            return carry

        lax.fori_loop(0, tiles, reduce_tile, 0, unroll=UNROLL)

    late = c >= middle
    after_last = (r == 0) & (c == 1)
    inner = x.at[:, 1 : tiles - 1, PAD : PAD + height]
    pltpu.make_async_copy(inner, inner, x_sem.at[2]).wait()
    for b in range(bands):
        reduce_band(b)
    pl.when(jnp.logical_not(late | direct))(forward)

    rest = sum(sizes[1:])
    at = lax.broadcasted_iota(jnp.int32, (128, 128), 1)

    def reduce_columns(b):
        base = 0
        for k in range(LEVELS):
            for i in range(tiles):
                high, low = split(ys[k][b, i, PAD : PAD + sizes[k]])
                if k == 0:
                    h, lanes = divmod(128 * i, half)
                    s1[2 * h * sizes[0] : (2 * h + 1) * sizes[0], lanes : lanes + 128] = high
                    s1[(2 * h + 1) * sizes[0] : (2 * h + 2) * sizes[0], lanes : lanes + 128] = low
                else:
                    s234[base : base + sizes[k], 128 * i : 128 * i + 128] = high
                    s234[rest + base : rest + base + sizes[k], 128 * i : 128 * i + 128] = low
            base += sizes[k] if k else 0
        one = dot(s1[...], c1[...])
        size = sizes[0]
        one = across_middle(
            (one[:size] + one[size : 2 * size], one[2 * size : 3 * size] + one[3 * size :]),
            y1[b, tiles // 2 - 1, PAD : PAD + size],
            y1[b, tiles // 2, PAD : PAD + size],
        )
        o1[b, :, : half // 2] = one[0]
        o1[b, :, half // 2 :] = one[1]
        two = dot(s234[...], c12[...])
        two = two[:rest] + two[rest:]
        three = dot_split(two[sizes[1] :], c3[...])
        four = dot_split(three[sizes[2] :], c4[...])
        o2[b] = two[: sizes[1]]
        o3[b] = three[: sizes[2]]
        o4[b] = four[:, : width >> 4]
    for b in range(bands):
        reduce_columns(b)

    @pl.when(direct)
    def _():
        v_low.wait_recv()
        for b in range(bands):
            vown[b] = vown[b] + jnp.where(row == 7, pltpu.roll(vfrom_high[...], 7 - b, 0), 0.0)

    def finish_columns(b):
        for part, levels in ((0, (0,)), (1, (1, 2, 3))):
            square = jnp.concatenate(
                [vown[b, :, 128 * part : 128 * part + 128], jnp.zeros((120, 128), jnp.float32)], 0
            ).T
            for k in levels:
                out = (o1, o2, o3, o4)[k]
                begin = starts[k] - 128 * part
                value = square[begin : begin + sizes[k]]
                tile = min(out.shape[2], 128)
                mark = at[: sizes[k]]
                low_cells = jnp.where(mark < 2, value, 0.0)[:, :tile]
                high_cells = jnp.where(mark == tile - 1, pltpu.roll(value, tile - 8, 1), 0.0)[:, :tile]
                out[b, :, 0:tile] = out[b, :, 0:tile] + low_cells
                out[b, :, out.shape[2] - tile :] = out[b, :, out.shape[2] - tile :] + high_cells
    for b in range(bands):
        finish_columns(b)

    above = lax.broadcasted_iota(jnp.int32, (8, 128), 1) < 8
    z_arrive()
    for b in range(bands):
        low_rows[b] = jnp.where(has_low_row, zfrom_low[b], 0.0)
        high_rows[b] = jnp.where(has_high_row, zfrom_high[b], 0.0)
    e_arrive()
    from_low, from_high = direct & has_low_row, direct & has_high_row
    pl.when(from_low)(diagonals[0].wait_recv)
    pl.when(from_high)(diagonals[1].wait_recv)
    diagonal = jnp.where(
        above, jnp.where(from_low, dfrom_low[...], 0.0), jnp.where(from_high, dfrom_high[...], 0.0)
    )
    last_row = lax.broadcasted_iota(jnp.int32, (8, 128), 0) == 7
    for b in range(bands):
        corners[b] = jnp.where(
            above,
            jnp.where(has_low_row, efrom_low[b], 0.0),
            jnp.where(has_high_row, efrom_high[b], 0.0),
        ) + jnp.where(last_row, pltpu.roll(diagonal, 7 - b, 0), 0.0)
    pl.when(sends_diagonal & has_high_row)(diagonals[0].wait_send)
    pl.when(sends_diagonal & has_low_row)(diagonals[1].wait_send)
    e_sent()
    z_sent()
    v_sent()


def store_kernel(a1, a2, a3, a4, low_rows, high_rows, corners, o1, o2, o3, o4, t1, t2, t3, t4, in_sem, edge_sem):
    bands = a1.shape[0]
    copies = []
    for k, (source, target) in enumerate(((a1, o1), (a2, o2), (a3, o3))):
        inner = slice(8, source.shape[1] - 8)
        copies.append(pltpu.make_async_copy(source.at[:, inner], target.at[:, inner], in_sem.at[k]))
        copies[-1].start()
    lane = lax.broadcasted_iota(jnp.int32, (16, 128), 1)
    for b in range(bands):
        cells = jnp.concatenate([corners[b], jnp.zeros((120, 128), jnp.float32)], 0).T[:16]
        first = jnp.where(lane < 2, cells, 0.0)
        last = jnp.where(lane == 127, pltpu.roll(cells, 120, 1), 0.0)
        last_half = jnp.where(lane == 63, pltpu.roll(cells, 56, 1), 0.0)
        for side, rows in enumerate((low_rows[b], high_rows[b])):
            for k, (source, target) in enumerate(zip((a1, a2, a3, a4), (t1, t2, t3, t4))):
                size, wide = source.shape[1:]
                count = 2 if side == 0 and k > 0 else 1
                at = slice(8 * side + 2 * k, 8 * side + 2 * k + count)
                if k == 0:
                    none = jnp.zeros((1, wide - 256), jnp.float32)
                    more = jnp.concatenate([rows[0:1], rows[1:2]], 1)
                    more = more + jnp.concatenate([first[at], none, last[at]], 1)
                else:
                    more = rows[2 * k : 2 * k + count, :wide]
                    if k == 1:
                        more = more + jnp.concatenate([first[at], last[at]], 1)
                    elif k == 2:
                        more = more + first[at] + last[at]
                    else:
                        more = more + (first[at] + last_half[at])[:, :wide]
                still = jnp.zeros((8 - count, wide), jnp.float32)
                if side == 0:
                    target[side, b] = source[b, 0:8] + jnp.concatenate([more, still], 0)
                else:
                    target[side, b] = source[b, size - 8 : size] + jnp.concatenate([still, more], 0)
    for k, (source, target) in enumerate(((t1, o1), (t2, o2), (t3, o3), (t4, o4))):
        size = target.shape[1]
        for side, begin in enumerate((0, size - 8)):
            pltpu.make_async_copy(source.at[side], target.at[:, begin : begin + 8], edge_sem.at[k]).start()
        copies.append(pltpu.make_async_copy(source, source, edge_sem.at[k]))
    for copy in copies:
        copy.wait()


def solution(mesh):
    rows_n, cols_n = mesh.shape["row"], mesh.shape["col"]
    row_table, col_table = tables()
    all_rows = whole_rows(256)

    def local(relief):
        bands, height, width = relief.shape
        f32, bf16 = jnp.float32, jnp.bfloat16
        c1 = reduce_matrix(width // 2, False).T
        c12 = chain(width, False)[1].T
        c3 = reduce_matrix(width // 4, False).T
        c4 = np.zeros((width // 4, 128))
        c4[: width // 8, : width // 16] = reduce_matrix(width // 8, False).T
        cc = np.concatenate([c12, c1, np.concatenate([c3, c4], 1)], 0)
        consts = [jnp.asarray(a, bf16) for a in (row_table, col_table, all_rows, cc)]
        shapes = [(bands, height >> k, width >> k) for k in range(1, LEVELS + 1)]

        vmem = lambda *shape, dtype=f32: pltpu.VMEM(shape, dtype)
        scratch = [vmem(bands, 2 * ROW_STRIP, width)]
        scratch += [vmem(bands, width // 128, (height >> k) + 2 * PAD, 128) for k in range(LEVELS + 1)]
        rest = sum(height >> k for k in range(2, LEVELS + 1))
        scratch += [
            vmem(2 * height, width // 2, dtype=bf16), vmem(2 * rest, width, dtype=bf16),
        ]
        scratch += [vmem(*a.shape, dtype=bf16) for a in (row_table[0], col_table[0], all_rows[0], cc)]
        scratch += [vmem(bands, width // 128, 16, 128)]
        scratch += [vmem(bands, 8, width // 4)] * 4
        scratch += [vmem(bands, 8, 128)] * 3
        scratch += [vmem(bands, 8, height + 128)] + [vmem(8, height + 128)] * 4
        scratch += [vmem(8, 128)] * 2
        scratch += [
            pltpu.SemaphoreType.DMA(n) for n in ((), (3,), (4,), (4,), (4,), (4,), (4,))
        ]
        scratch += [pltpu.SemaphoreType.REGULAR]
        extra = [(bands, 8, width // 4)] * 2 + [(bands, 8, 128)]
        held = pl.pallas_call(
            functools.partial(pyramid_kernel, rows_n, cols_n),
            out_shape=[jax.ShapeDtypeStruct(s, f32) for s in shapes + extra],
            in_specs=[pl.BlockSpec(memory_space=pltpu.HBM)] * 5,
            out_specs=[pl.BlockSpec(memory_space=pltpu.VMEM)] * (LEVELS + 3),
            scratch_shapes=scratch,
            compiler_params=pltpu.CompilerParams(
                collective_id=0, has_side_effects=True, vmem_limit_bytes=40 << 20
            ),
            name="pyramid",
        )(*[pltpu.with_memory_space_constraint(a, pltpu.HBM) for a in (relief, *consts)])
        return pl.pallas_call(
            store_kernel,
            out_shape=[jax.ShapeDtypeStruct(s, f32) for s in shapes],
            in_specs=[pl.BlockSpec(memory_space=pltpu.VMEM)] * (LEVELS + 3),
            out_specs=[pl.BlockSpec(memory_space=pltpu.HBM)] * LEVELS,
            scratch_shapes=[vmem(2, bands, 8, across) for _, _, across in shapes]
            + [pltpu.SemaphoreType.DMA((LEVELS - 1,)), pltpu.SemaphoreType.DMA((LEVELS,))],
            compiler_params=pltpu.CompilerParams(vmem_limit_bytes=16 << 20),
            name="store",
        )(*held)

    spec = P(None, "row", "col")
    return jax.shard_map(local, mesh=mesh, in_specs=(spec,), out_specs=(spec,) * LEVELS, check_vma=False)
```
